256 devices in a mesh: orient: 16 (over z, y_hi), trow: 4 (over y_lo, core), tcol: 4 (over x).
Axes of the slice: x: 4, y: 4 (y_hi: 2, y_lo: 2; y = y_hi * 2 + y_lo), z: 8, core: 2. Of those that a mesh axis runs over, the one named last changes fastest.
Arguments:
- micrograph: float32 [512, 512], P('trow', 'tcol'), may hold values from -6 to 6
- templates: float32 [16, 256, 256], P('orient'), may hold values from -600 to 600
- fine_templates: float32 [256, 256, 256], P('orient'), may hold values from -600 to 600
- peak_rows: int32 [256], P(('trow', 'tcol')), may hold values from 0 to 127
- peak_cols: int32 [256], P(('trow', 'tcol')), may hold values from 0 to 127
- peak_count: int32 [16], P(('trow', 'tcol')), may hold values from 1 to 16, 128 in all
Outputs:
- snr_map: float32 [512, 512], P('trow', 'tcol')
- refined: float32 [256], P(('trow', 'tcol'))
The draws below stay inside these ranges and needn't reach their ends.
Inputs may be any that keep to these rules, and one draw needn't show every extreme that they name: The live slots of tile g are its first peak_count[g] slots; the counts of all tiles sum to 128.
All inputs are finite; a program needn't handle non-finite values. No bound on the sum of `peak_count` on one device may be relied on, other than what follows from the above.
Results may differ from the reference program's by a relative error of at most 0.00027.
Values sent between devices are 32-bit elements; how exact they have to be, the bound alone decides.
A program may use at most 64 MiB of HBM per device.

```python
import math
import jax
import jax.numpy as jnp
import numpy as np
from jax import lax

TILE = 128
PROJ = 256
PEAK_AVG = 8
PEAK_CAP = 16
TILES = 16
ORIENT = 16
FINE = 256
NY = 512
NX = 512
PEAKS = 256
N_TCOL = 4


def shaped_stack(key, number):
    keys = jax.random.split(key, 4)
    row_scale = jnp.exp(jax.random.uniform(keys[0], (number, PROJ, 1), jnp.float32, 0.0, math.log(10.0)))
    col_scale = jnp.exp(jax.random.uniform(keys[1], (number, 1, PROJ), jnp.float32, 0.0, math.log(10.0)))
    base = jnp.clip(jax.random.normal(keys[3], (number, PROJ, PROJ), jnp.float32), -6.0, 6.0)
    return base * row_scale * col_scale


def draw_templates(key, part):
    return shaped_stack(jax.random.fold_in(key, 11), ORIENT)


def draw_fine_templates(key, part):
    return shaped_stack(jax.random.fold_in(key, 23), FINE)


def plant(values, stream_key, least, high):
    longest = values.shape.index(max(values.shape))
    spots = []
    for shift in (0, 1):
        where = [jax.random.randint(jax.random.fold_in(stream_key, axis), (), 0, length) for axis, length in enumerate(values.shape)]
        where[longest] = (where[longest] + shift) % values.shape[longest]
        spots.append(tuple(where))
    return values.at[spots[0]].set(least).at[spots[1]].set(high)


def shard_levels(rng, shape, cuts, low, largest):
    gain = 1.0
    for dim, parts in cuts:
        heights = jax.random.uniform(jax.random.fold_in(jax.random.fold_in(rng, 6), dim), (parts,), jnp.float32, low / len(cuts), largest / len(cuts))
        gain = gain * jnp.repeat(jnp.exp(heights), shape[dim] // parts).reshape((-1,) + (1,) * (len(shape) - 1 - dim))
    return gain


def profile(amount, total, bound, skew):
    portions = [(1 << 20) // math.isqrt(grade ** skew) + 1 for grade in range(2, amount + 1)]
    rest, counts = total - bound - (amount - 1), [1] * (amount - 1)
    while rest > 0:
        candidates = [i for i in range(amount - 1) if counts[i] < bound]
        pool, budget = sum([portions[i] for i in candidates]), rest
        for i in candidates:
            more = min(bound - counts[i], max(1, budget * portions[i] // pool), rest)
            counts[i] = counts[i] + more
            rest = rest - more
    return np.array([bound] + counts)


def ragged_sizes(key, number_of, total, limit, skew):
    if number_of == 2:
        one = jax.random.randint(key, (), max(1, total - limit), min(limit, total - 1) + 1)
        return jnp.stack([one, total - one])
    tallies = jnp.asarray(profile(number_of, total, limit, skew), jnp.int32)
    twos = (number_of - 1) // 2
    source_of, taker = tallies[1:1 + 2 * twos:2], tallies[2:2 + 2 * twos:2]
    room = jnp.minimum(source_of - 1, limit - taker)
    passed = jax.random.randint(jax.random.fold_in(key, 1), (twos,), 0, 1 << 20) % (room + 1)
    tallies = tallies.at[1:1 + 2 * twos:2].set(source_of - passed).at[2:2 + 2 * twos:2].set(taker + passed)
    return tallies[jax.random.permutation(jax.random.fold_in(key, 2), number_of)]


def noise(rng, shape, deviation, most, shards=(), kind=jnp.bfloat16):
    result = jax.random.normal(rng, shape, jnp.float32) * deviation
    if len(shards) > 0:
        result = shard_levels(rng, shape, shards, -0.22, 0.18) * result
    return jnp.clip(result, min=-most, max=most).astype(kind)


def setup_inputs(seed: int = 0) -> dict:
    streams_of = jax.random.split(jax.random.key(seed), 7)
    micrograph = noise(streams_of[0], (NY, NX), 1.0, 6.0, ((0, 4), (1, 4)), jnp.float32)
    templates = draw_templates(jax.random.fold_in(streams_of[6], 71), 0)
    fine_templates = draw_fine_templates(jax.random.fold_in(streams_of[6], 71), 0)
    peak_rows = plant(jax.random.randint(streams_of[3], (PEAKS,), 0, TILE), jax.random.fold_in(streams_of[3], 1), 0, TILE - 1).astype(jnp.int32)
    peak_cols = plant(jax.random.randint(streams_of[4], (PEAKS,), 0, TILE), jax.random.fold_in(streams_of[4], 1), 0, TILE - 1).astype(jnp.int32)
    peak_count = ragged_sizes(streams_of[5], TILES, PEAK_AVG * TILES, PEAK_CAP, 2).astype(jnp.int32)
    return dict(micrograph=micrograph, templates=templates, fine_templates=fine_templates, peak_rows=peak_rows, peak_cols=peak_cols, peak_count=peak_count)


def normalize(stack):
    centered = stack - lax.optimization_barrier(jnp.mean(stack, axis=(1, 2), keepdims=True))
    spread = lax.optimization_barrier(jnp.mean(centered * centered, axis=(1, 2), keepdims=True))
    return centered / jnp.sqrt(spread + 1e-06)

def reference(micrograph, templates, fine_templates, peak_rows, peak_cols, peak_count):
    half_width = PROJ // 2
    height, width = micrograph.shape
    padded = jnp.pad(micrograph, ((half_width, half_width), (half_width, half_width)))
    spectrum = jnp.fft.rfft2(padded)
    normed = normalize(templates)

    def correlate(state, template):
        tspec = jnp.fft.rfft2(template, s=padded.shape)
        correl = jnp.fft.irfft2(spectrum * jnp.conj(tspec), s=padded.shape)[:height, :width] / PROJ
        best_map, total_map, squares = state
        return ((jnp.maximum(best_map, correl), total_map + correl, squares + correl * correl), None)
    start = (jnp.full((height, width), -1e+30, dtype=jnp.float32), jnp.zeros((height, width), jnp.float32), jnp.zeros((height, width), jnp.float32))
    (best_map, total_map, squares), _ = lax.scan(correlate, start, normed)
    orient_count = templates.shape[0]
    snr_map = (best_map - total_map / orient_count) / jnp.sqrt(squares / orient_count + 1e-05)
    fine_flat = normalize(fine_templates).reshape(fine_templates.shape[0], PROJ * PROJ)
    slot_ids = jnp.arange(PEAKS, dtype=jnp.int32)
    tile_ids = slot_ids // PEAK_CAP
    global_rows = tile_ids // N_TCOL * TILE + peak_rows
    global_cols = tile_ids % N_TCOL * TILE + peak_cols

    def extract(row_start, col_start):
        return lax.dynamic_slice(padded, (row_start, col_start), (PROJ, PROJ))
    patches = jax.vmap(extract)(global_rows, global_cols).reshape(PEAKS, PROJ * PROJ)
    scores = jnp.dot(patches, fine_flat.T, precision=lax.Precision.HIGHEST, preferred_element_type=jnp.float32) / PROJ
    best_fine = lax.optimization_barrier(jnp.max(scores, axis=1))
    live_slots = slot_ids % PEAK_CAP < peak_count[tile_ids]
    refined = jnp.where(live_slots, best_fine, 0.0)
    return (snr_map, refined)
```

```python
import jax
import jax.numpy as jnp
import numpy as np
from jax import lax
from jax.experimental import pallas as pl
from jax.experimental.pallas import tpu as pltpu
from jax.sharding import PartitionSpec as P

F32 = jnp.float32
BF16 = jnp.bfloat16
MESH = pl.DeviceIdType.MESH
T = 128
LEN = 3 * T
PROJ = 2 * T
GROUP = 16
SLOTS = 16
FINE = 16
HALF_ROOT3 = float(np.sqrt(3.0) / 2.0)
NEAR = [(dr, dc) for dr in (-1, 0, 1) for dc in (-1, 0, 1) if (dr, dc) != (0, 0)]
FAR_FIRST = (8, 7, 9, 6, 10, 5, 11, 4, 12, 3, 13, 1, 15, 2, 14)


def hi_lo(table):
    high = table.astype(BF16)
    low = (table - high.astype(np.float64)).astype(BF16)
    return np.stack([high, low])


def tables():
    b = np.arange(T)
    q = np.arange(T)
    k0 = 3 * q + 0.5
    k1 = 3 * np.arange(T // 2) + 1.5
    unit = 2.0 * np.pi / LEN
    a0 = unit * np.outer(b, k0)
    a1 = unit * np.outer(b, k1)
    row0 = np.block([[np.cos(a0), -np.sin(a0)], [np.sin(a0), np.cos(a0)]])
    row1 = np.concatenate([np.cos(a1), -np.sin(a1)], 1)
    col, inv = [], []
    for r in range(3):
        th = unit * np.outer(3 * q + r, b)
        col.append(np.concatenate([np.cos(th), np.sin(th)], 1))
        inv.append(np.concatenate([np.cos(th).T, -np.sin(th).T], 1))
    back = np.concatenate([np.cos(a0).T, -np.sin(a0).T, np.cos(a1).T, -np.sin(a1).T], 0)
    back = back * (2.0 / (LEN * LEN * PROJ))
    return (
        hi_lo(row0),
        hi_lo(row1),
        hi_lo(np.stack(col)),
        hi_lo(np.stack(inv)),
        hi_lo(back),
    )


def split(x):
    high = x.astype(BF16)
    return high, (x - high.astype(F32)).astype(BF16)


def dot(a, b):
    return jnp.dot(a, b, preferred_element_type=F32)


def table_times(high, low, x):
    xh, xl = split(x)
    return dot(high, xh) + dot(low, xh) + dot(high, xl)


def times_table(x, high, low):
    xh, xl = split(x)
    return dot(xh, high) + dot(xl, high) + dot(xh, low)


def rotated(z):
    last = z[:, 2 * T :]
    lane = lax.broadcasted_iota(jnp.int32, last.shape, 1)
    turned = pltpu.roll(last, T // 2, 1)
    turned = jnp.where(lane < T // 2, turned, -turned)
    return jnp.concatenate([z[:, T : 2 * T], -z[:, :T], turned], axis=1)


def with_rotated(z):
    return jnp.concatenate([z, rotated(z)], axis=0)


def kernel(
    tile, template, fine, rows, cols, row0, row1, col, inv, back,
    snr_out, best_out,
    win, tmpl, fine_v, row0_v, row1_v, col_v, inv_v, back_v, spec,
    scale, patch, acc, corr, bands, snr, finals,
    load_sem, halo_send, halo_recv, band_send, band_recv,
    snr_send, snr_recv, final_send, final_recv, near_sem, mid_sem, far_sem,
):
    o = lax.axis_index("orient")
    r = lax.axis_index("trow")
    c = lax.axis_index("tcol")

    loads = [
        pltpu.make_async_copy(src, dst, load_sem.at[i])
        for i, (src, dst) in enumerate(
            [
                (template.at[0], tmpl),
                (row0, row0_v),
                (row1, row1_v),
                (col, col_v),
                (tile, win.at[1, pl.ds(T, T)]),
                (fine, fine_v),
                (inv, inv_v),
                (back, back_v),
            ]
        )
    ]
    for load in loads:
        load.start()

    def other(step):
        return lax.rem(o + (step % GROUP), GROUP)

    def inside(dr, dc):
        checks = []
        if dr < 0:
            checks.append(r > 0)
        if dr > 0:
            checks.append(r < 3)
        if dc < 0:
            checks.append(c > 0)
        if dc > 0:
            checks.append(c < 3)
        out = checks[0]
        for check in checks[1:]:
            out = jnp.logical_and(out, check)
        return out

    mate = o + 1 - 2 * lax.rem(o, 2)
    barrier = pltpu.get_barrier_semaphore()
    for dr, dc in NEAR:
        @pl.when(inside(dr, dc))
        def _():
            pl.semaphore_signal(barrier, inc=1, device_id=(o, r + dr, c + dc), device_id_type=MESH)
    for peer in (other(2), other(14), mate):
        pl.semaphore_signal(barrier, inc=1, device_id=(peer, r, c), device_id_type=MESH)
    across = 3 - (r == 0).astype(jnp.int32) - (r == 3).astype(jnp.int32)
    along = 3 - (c == 0).astype(jnp.int32) - (c == 3).astype(jnp.int32)
    pl.semaphore_wait(barrier, across * along + 2)

    def halo(i):
        dr, dc = NEAR[i]
        return pltpu.make_async_remote_copy(
            src_ref=tile,
            dst_ref=win.at[1 - dc, pl.ds((1 - dr) * T, T)],
            send_sem=halo_send.at[i],
            recv_sem=halo_recv.at[i],
            device_id=(o, r + dr, c + dc),
            device_id_type=MESH,
        )

    for i, (dr, dc) in enumerate(NEAR):
        @pl.when(inside(dr, dc))
        def _():
            halo(i).start()

        @pl.when(jnp.logical_not(inside(dr, dc)))
        def _():
            win[1 + dc, pl.ds((1 + dr) * T, T)] = jnp.zeros((T, T), F32)

    for peer in (other(2), other(14)):
        pl.semaphore_signal(near_sem, inc=1, device_id=(peer, r, c), device_id_type=MESH)

    def row_dft(x0, x1, x2):
        if x2 is None:
            mixed = jnp.concatenate([x0 + 0.5 * x1, -HALF_ROOT3 * x1], axis=1)
            real = x0 - x1
        else:
            mixed = jnp.concatenate([x0 + 0.5 * (x1 - x2), -HALF_ROOT3 * (x1 + x2)], axis=1)
            real = x0 - x1 + x2
        return jnp.concatenate(
            [times_table(mixed, row0_v[0], row0_v[1]), times_table(real, row1_v[0], row1_v[1])], axis=1
        )

    def col_dft(b0, b1, b2):
        if b2 is None:
            total = b0 + b1
            even = b0 - 0.5 * b1
            odd = rotated(HALF_ROOT3 * b1)
        else:
            total = b0 + (b1 + b2)
            even = b0 - 0.5 * (b1 + b2)
            odd = rotated(HALF_ROOT3 * (b1 - b2))
        for k, z in enumerate((total, even + odd, even - odd)):
            yield table_times(col_v[0, k], col_v[1, k], with_rotated(z))

    for load in loads[:4]:
        load.wait()
    t = tmpl[...]
    t = t - jnp.sum(t, keepdims=True) * (1.0 / (PROJ * PROJ))
    spread = jnp.sum(t * t, keepdims=True) * (1.0 / (PROJ * PROJ))
    t = t / jnp.sqrt(spread + 1e-6)
    t = row_dft(t[:, :T], t[:, T:], None)
    for k, z in enumerate(col_dft(t[:T], t[T:], None)):
        spec[k] = z

    pl.semaphore_wait(near_sem, 2)
    for peer in (other(4), other(12)):
        pl.semaphore_signal(mid_sem, inc=1, device_id=(peer, r, c), device_id_type=MESH)

    loads[5].wait()

    @pl.loop(0, FINE)
    def _(f):
        t = fine_v[f]
        t = t - jnp.sum(t, keepdims=True) * (1.0 / (PROJ * PROJ))
        spread = jnp.sum(t * t, keepdims=True) * (1.0 / (PROJ * PROJ))
        fine_v[f] = t
        scale[pl.ds(f, 1)] = jnp.broadcast_to((1.0 / PROJ) / jnp.sqrt(spread + 1e-6), (1, T))

    pl.semaphore_wait(mid_sem, 2)
    pl.semaphore_signal(far_sem, inc=1, device_id=(other(8), r, c), device_id_type=MESH)

    loads[4].wait()
    loads[6].wait()
    loads[7].wait()
    for i, (dr, dc) in enumerate(NEAR):
        @pl.when(inside(-dr, -dc))
        def _():
            halo(i).wait_recv()

    w = row_dft(win[0], win[1], win[2])
    total = jnp.zeros((T, LEN), F32)
    lane = lax.broadcasted_iota(jnp.int32, (T, T), 1)
    for k, z in enumerate(col_dft(w[:T], w[T : 2 * T], w[2 * T :])):
        s = spec[k]
        last = s[:, 2 * T :]
        turned = pltpu.roll(last, T // 2, 1)
        re = jnp.concatenate([s[:, :T], s[:, :T], jnp.where(lane < T // 2, last, turned)], axis=1)
        im = jnp.concatenate(
            [s[:, T : 2 * T], s[:, T : 2 * T], jnp.where(lane < T // 2, turned, last)], axis=1
        )
        prod = z * re + rotated(z) * im
        total = total + table_times(inv_v[0, k], inv_v[1, k], with_rotated(prod))
    corr[...] = times_table(total, back_v[0], back_v[1]).reshape(GROUP, 8, T)

    pl.semaphore_wait(far_sem, 1)

    def band_copy(step, owner):
        return pltpu.make_async_remote_copy(
            src_ref=corr.at[other(step)],
            dst_ref=bands.at[owner],
            send_sem=band_send.at[step],
            recv_sem=band_recv.at[step],
            device_id=(other(step), r, c),
            device_id_type=MESH,
        )

    def spread_copy(buffer, sends, recvs, step, owner):
        return pltpu.make_async_remote_copy(
            src_ref=buffer.at[owner],
            dst_ref=buffer.at[owner],
            send_sem=sends.at[step],
            recv_sem=recvs.at[step],
            device_id=(other(step), r, c),
            device_id_type=MESH,
        )

    for step in FAR_FIRST:
        band_copy(step, o).start()
    bands[o] = corr[o]

    fine_lane = lax.broadcasted_iota(jnp.int32, (PROJ, T), 1)

    @pl.loop(0, SLOTS // 4)
    def _(block):
        for k in range(4):
            row = rows[block * 4 + k]
            column = cols[block * 4 + k]
            shift = lax.rem(T - column, T)
            parts = [pltpu.roll(win[j, pl.ds(row, PROJ)], shift, 1) for j in range(3)]
            for j in range(2):
                patch[k, j] = jnp.where(fine_lane < T - column, parts[j], parts[j + 1])

        @pl.loop(0, FINE // 4)
        def _(group):
            def step(i, sums):
                sums = list(sums)
                at = pl.ds(pl.multiple_of(i * 8, 8), 8)
                for j in range(2):
                    ps = [patch[k, j, at] for k in range(4)]
                    for m in range(4):
                        t = fine_v[group * 4 + m, at, pl.ds(j * T, T)]
                        for k in range(4):
                            sums[k * 4 + m] = sums[k * 4 + m] + ps[k] * t
                return tuple(sums)

            sums = lax.fori_loop(
                0, PROJ // 8, step, tuple(jnp.zeros((8, T), F32) for _ in range(16)), unroll=2
            )
            for k in range(4):
                for m in range(4):
                    acc[(block * 4 + k) * FINE + group * 4 + m] = sums[k * 4 + m]

    scores = jnp.sum(acc[...], axis=1).reshape(SLOTS, FINE, T) * scale[...][None]
    scores = jnp.sum(scores, axis=2, keepdims=True)
    local = jnp.broadcast_to(jnp.max(scores, axis=1), (SLOTS, T))
    at_row = lax.broadcasted_iota(jnp.int32, (SLOTS, T), 0)
    at_lane = lax.broadcasted_iota(jnp.int32, (SLOTS, T), 1)
    local = jnp.sum(jnp.where(at_row == at_lane, local, 0.0), axis=0, keepdims=True)
    finals[o] = jnp.broadcast_to(local, (8, T))
    for step in FAR_FIRST:
        spread_copy(finals, final_send, final_recv, step, o).start()

    for step in FAR_FIRST:
        band_copy(step, other(-step)).wait_recv()
    best = bands[0]
    added = bands[0]
    squares = bands[0] * bands[0]
    for k in range(1, GROUP):
        value = bands[k]
        best = jnp.maximum(best, value)
        added = added + value
        squares = squares + value * value
    snr[o] = (best - added / GROUP) / jnp.sqrt(squares / GROUP + 1e-5)
    for step in FAR_FIRST:
        spread_copy(snr, snr_send, snr_recv, step, o).start()

    for step in FAR_FIRST:
        spread_copy(finals, final_send, final_recv, step, other(-step)).wait_recv()
    best_fine = finals[0]
    for k in range(1, GROUP):
        best_fine = jnp.maximum(best_fine, finals[k])
    best_out[...] = best_fine

    for step in FAR_FIRST:
        spread_copy(snr, snr_send, snr_recv, step, other(-step)).wait_recv()
    snr_out[...] = snr[...].reshape(T, T)

    for i, (dr, dc) in enumerate(NEAR):
        @pl.when(inside(dr, dc))
        def _():
            halo(i).wait_send()
    for step in FAR_FIRST:
        band_copy(step, o).wait_send()
        spread_copy(finals, final_send, final_recv, step, o).wait_send()
        spread_copy(snr, snr_send, snr_recv, step, o).wait_send()


def per_device(micrograph, templates, fine_templates, peak_rows, peak_cols, peak_count):
    consts = [jnp.asarray(x) for x in tables()]
    any_spec = pl.BlockSpec(memory_space=pl.ANY)
    smem = pl.BlockSpec(memory_space=pltpu.SMEM)
    vmem = pl.BlockSpec(memory_space=pltpu.VMEM)
    dma = pltpu.SemaphoreType.DMA
    regular = pltpu.SemaphoreType.REGULAR
    snr, best = pl.pallas_call(
        kernel,
        out_shape=(
            jax.ShapeDtypeStruct((T, T), F32),
            jax.ShapeDtypeStruct((8, T), F32),
        ),
        in_specs=[any_spec] * 3 + [smem] * 2 + [any_spec] * 5,
        out_specs=(vmem, vmem),
        scratch_shapes=[
            pltpu.VMEM((3, LEN, T), F32),
            pltpu.VMEM((PROJ, PROJ), F32),
            pltpu.VMEM((FINE, PROJ, PROJ), F32),
            pltpu.VMEM((2, 2 * T, 2 * T), BF16),
            pltpu.VMEM((2, T, T), BF16),
            pltpu.VMEM((2, 3, T, 2 * T), BF16),
            pltpu.VMEM((2, 3, T, 2 * T), BF16),
            pltpu.VMEM((2, LEN, T), BF16),
            pltpu.VMEM((3, T, LEN), F32),
            pltpu.VMEM((FINE, T), F32),
            pltpu.VMEM((4, 2, PROJ, T), F32),
            pltpu.VMEM((SLOTS * FINE, 8, T), F32),
            pltpu.VMEM((GROUP, 8, T), F32),
            pltpu.VMEM((GROUP, 8, T), F32),
            pltpu.VMEM((GROUP, 8, T), F32),
            pltpu.VMEM((GROUP, 8, T), F32),
            dma((8,)),
            dma((8,)),
            dma((8,)),
            dma((16,)),
            dma((16,)),
            dma((16,)),
            dma((16,)),
            dma((16,)),
            dma((16,)),
            regular,
            regular,
            regular,
        ],
        compiler_params=pltpu.CompilerParams(
            collective_id=0, has_side_effects=True
        ),
    )(micrograph, templates, fine_templates, peak_rows, peak_cols, *consts)
    slots = jnp.arange(SLOTS, dtype=jnp.int32)
    refined = jnp.where(slots < peak_count[0], best[0, :SLOTS], 0.0)
    return snr, refined


def solution(mesh):
    placed = (
        P("trow", "tcol"),
        P("orient", None, None),
        P("orient", None, None),
        P(("trow", "tcol")),
        P(("trow", "tcol")),
        P(("trow", "tcol")),
    )
    return jax.shard_map(
        per_device,
        mesh=mesh,
        in_specs=placed,
        out_specs=(P("trow", "tcol"), P(("trow", "tcol"))),
        check_vma=False,
    )
```

```python
import jax
import jax.numpy as jnp
import numpy as np
from jax import lax
from jax.experimental import pallas as pl
from jax.experimental.pallas import tpu as pltpu
from jax.sharding import PartitionSpec as P

F32 = jnp.float32
BF16 = jnp.bfloat16
MESH = pl.DeviceIdType.MESH
T = 128
LEN = 3 * T
PROJ = 2 * T
GROUP = 16
SLOTS = 16
FINE = 16
HALF_ROOT3 = float(np.sqrt(3.0) / 2.0)
NEAR = [(dr, dc) for dr in (-1, 0, 1) for dc in (-1, 0, 1) if (dr, dc) != (0, 0)]
FAR_FIRST = (8, 7, 9, 6, 10, 5, 11, 4, 12, 3, 13, 1, 15, 2, 14)


def hi_lo(table):
    high = table.astype(BF16)
    low = (table - high.astype(np.float64)).astype(BF16)
    return np.stack([high, low])


def tables():
    b = np.arange(T)
    q = np.arange(T)
    k0 = 3 * q + 0.5
    k1 = 3 * np.arange(T // 2) + 1.5
    unit = 2.0 * np.pi / LEN
    a0 = unit * np.outer(b, k0)
    a1 = unit * np.outer(b, k1)
    row0 = np.block([[np.cos(a0), -np.sin(a0)], [np.sin(a0), np.cos(a0)]])
    row1 = np.concatenate([np.cos(a1), -np.sin(a1)], 1)
    col, inv = [], []
    for r in range(3):
        th = unit * np.outer(3 * q + r, b)
        col.append(np.concatenate([np.cos(th), np.sin(th)], 1))
        inv.append(np.concatenate([np.cos(th).T, -np.sin(th).T], 1))
    back = np.concatenate([np.cos(a0).T, -np.sin(a0).T, np.cos(a1).T, -np.sin(a1).T], 0)
    back = back * (2.0 / (LEN * LEN * PROJ))
    return (
        hi_lo(row0),
        hi_lo(row1),
        hi_lo(np.stack(col)),
        hi_lo(np.stack(inv)),
        hi_lo(back),
    )


def split(x):
    high = x.astype(BF16)
    return high, (x - high.astype(F32)).astype(BF16)


def dot(a, b):
    return jnp.dot(a, b, preferred_element_type=F32)


def table_times(high, low, x):
    xh, xl = split(x)
    return dot(high, xh) + dot(low, xh) + dot(high, xl)


def times_table(x, high, low):
    xh, xl = split(x)
    return dot(xh, high) + dot(xl, high) + dot(xh, low)


def rotated(z):
    last = z[:, 2 * T :]
    lane = lax.broadcasted_iota(jnp.int32, last.shape, 1)
    turned = pltpu.roll(last, T // 2, 1)
    turned = jnp.where(lane < T // 2, turned, -turned)
    return jnp.concatenate([z[:, T : 2 * T], -z[:, :T], turned], axis=1)


def with_rotated(z):
    return jnp.concatenate([z, rotated(z)], axis=0)


def kernel(
    tile, template, fine, rows, cols, row0, row1, col, inv, back,
    snr_out, best_out,
    win, tmpl, fine_v, row0_v, row1_v, col_v, inv_v, back_v, spec,
    sums, squares_v, patches, planes, corr, bands, snr, finals,
    load_sem, halo_send, halo_recv, band_send, band_recv,
    snr_send, snr_recv, final_send, final_recv, near_sem, mid_sem, far_sem,
):
    o = lax.axis_index("orient")
    r = lax.axis_index("trow")
    c = lax.axis_index("tcol")

    loads = [
        pltpu.make_async_copy(src, dst, load_sem.at[i])
        for i, (src, dst) in enumerate(
            [
                (template.at[0], tmpl),
                (row0, row0_v),
                (row1, row1_v),
                (col, col_v),
                (tile, win.at[1, pl.ds(T, T)]),
                (fine, fine_v),
                (inv, inv_v),
                (back, back_v),
            ]
        )
    ]
    for load in loads:
        load.start()

    def other(step):
        return lax.rem(o + (step % GROUP), GROUP)

    def inside(dr, dc):
        checks = []
        if dr < 0:
            checks.append(r > 0)
        if dr > 0:
            checks.append(r < 3)
        if dc < 0:
            checks.append(c > 0)
        if dc > 0:
            checks.append(c < 3)
        out = checks[0]
        for check in checks[1:]:
            out = jnp.logical_and(out, check)
        return out

    mate = o + 1 - 2 * lax.rem(o, 2)
    barrier = pltpu.get_barrier_semaphore()
    for dr, dc in NEAR:
        @pl.when(inside(dr, dc))
        def _():
            pl.semaphore_signal(barrier, inc=1, device_id=(o, r + dr, c + dc), device_id_type=MESH)
    for peer in (other(2), other(14), mate):
        pl.semaphore_signal(barrier, inc=1, device_id=(peer, r, c), device_id_type=MESH)
    across = 3 - (r == 0).astype(jnp.int32) - (r == 3).astype(jnp.int32)
    along = 3 - (c == 0).astype(jnp.int32) - (c == 3).astype(jnp.int32)
    pl.semaphore_wait(barrier, across * along + 2)

    def halo(i):
        dr, dc = NEAR[i]
        return pltpu.make_async_remote_copy(
            src_ref=tile,
            dst_ref=win.at[1 - dc, pl.ds((1 - dr) * T, T)],
            send_sem=halo_send.at[i],
            recv_sem=halo_recv.at[i],
            device_id=(o, r + dr, c + dc),
            device_id_type=MESH,
        )

    for i, (dr, dc) in enumerate(NEAR):
        @pl.when(inside(dr, dc))
        def _():
            halo(i).start()

        @pl.when(jnp.logical_not(inside(dr, dc)))
        def _():
            win[1 + dc, pl.ds((1 + dr) * T, T)] = jnp.zeros((T, T), F32)

    for peer in (other(2), other(14)):
        pl.semaphore_signal(near_sem, inc=1, device_id=(peer, r, c), device_id_type=MESH)

    def row_dft(x0, x1, x2):
        if x2 is None:
            mixed = jnp.concatenate([x0 + 0.5 * x1, -HALF_ROOT3 * x1], axis=1)
            real = x0 - x1
        else:
            mixed = jnp.concatenate([x0 + 0.5 * (x1 - x2), -HALF_ROOT3 * (x1 + x2)], axis=1)
            real = x0 - x1 + x2
        return jnp.concatenate(
            [times_table(mixed, row0_v[0], row0_v[1]), times_table(real, row1_v[0], row1_v[1])], axis=1
        )

    def col_dft(b0, b1, b2):
        if b2 is None:
            total = b0 + b1
            even = b0 - 0.5 * b1
            odd = rotated(HALF_ROOT3 * b1)
        else:
            total = b0 + (b1 + b2)
            even = b0 - 0.5 * (b1 + b2)
            odd = rotated(HALF_ROOT3 * (b1 - b2))
        for k, z in enumerate((total, even + odd, even - odd)):
            yield table_times(col_v[0, k], col_v[1, k], with_rotated(z))

    for load in loads[:4]:
        load.wait()
    t = tmpl[...]
    t = t - jnp.sum(t, keepdims=True) * (1.0 / (PROJ * PROJ))
    spread = jnp.sum(t * t, keepdims=True) * (1.0 / (PROJ * PROJ))
    t = t / jnp.sqrt(spread + 1e-6)
    t = row_dft(t[:, :T], t[:, T:], None)
    for k, z in enumerate(col_dft(t[:T], t[T:], None)):
        spec[k] = z

    loads[5].wait()

    @pl.loop(0, FINE)
    def _(f):
        part = jnp.sum(fine_v[f].reshape(PROJ // 8, 8, PROJ), axis=0)
        sums[f] = part[:, :T] + part[:, T:]

    mean = jnp.sum(sums[...], axis=(1, 2), keepdims=True) * (1.0 / (PROJ * PROJ))
    sums[...] = jnp.broadcast_to(mean, (FINE, 8, T))

    pl.semaphore_wait(near_sem, 2)
    for peer in (other(4), other(12)):
        pl.semaphore_signal(mid_sem, inc=1, device_id=(peer, r, c), device_id_type=MESH)

    @pl.loop(0, FINE // 2)
    def _(pair):
        at = pl.ds(pl.multiple_of(pair * 16, 16), 16)
        below = pl.ds(pl.multiple_of(pair * 16 + T, 16), 16)
        mean = jnp.concatenate([sums[pair * 2], sums[pair * 2 + 1]], axis=0)
        mean = jnp.concatenate([mean, mean], axis=1)
        total = jnp.zeros((16, PROJ), F32)
        for i in range(PROJ // 8):
            group = pl.ds(i * 8, 8)
            x = jnp.concatenate([fine_v[pair * 2, group], fine_v[pair * 2 + 1, group]], axis=0) - mean
            total = total + x * x
            high, low = split(x)
            planes[at, pl.ds(i * PROJ, PROJ)] = high
            planes[below, pl.ds(i * PROJ, PROJ)] = low
        squares_v[at] = total[:, :T] + total[:, T:]

    pl.semaphore_wait(mid_sem, 2)
    pl.semaphore_signal(far_sem, inc=1, device_id=(other(8), r, c), device_id_type=MESH)

    loads[4].wait()
    loads[6].wait()
    loads[7].wait()
    for i, (dr, dc) in enumerate(NEAR):
        @pl.when(inside(-dr, -dc))
        def _():
            halo(i).wait_recv()

    w = row_dft(win[0], win[1], win[2])
    total = jnp.zeros((T, LEN), F32)
    lane = lax.broadcasted_iota(jnp.int32, (T, T), 1)
    for k, z in enumerate(col_dft(w[:T], w[T : 2 * T], w[2 * T :])):
        s = spec[k]
        last = s[:, 2 * T :]
        turned = pltpu.roll(last, T // 2, 1)
        re = jnp.concatenate([s[:, :T], s[:, :T], jnp.where(lane < T // 2, last, turned)], axis=1)
        im = jnp.concatenate(
            [s[:, T : 2 * T], s[:, T : 2 * T], jnp.where(lane < T // 2, turned, last)], axis=1
        )
        prod = z * re + rotated(z) * im
        total = total + table_times(inv_v[0, k], inv_v[1, k], with_rotated(prod))
    corr[...] = times_table(total, back_v[0], back_v[1]).reshape(GROUP, 8, T)

    pl.semaphore_wait(far_sem, 1)

    def band_copy(step, owner):
        return pltpu.make_async_remote_copy(
            src_ref=corr.at[other(step)],
            dst_ref=bands.at[owner],
            send_sem=band_send.at[step],
            recv_sem=band_recv.at[step],
            device_id=(other(step), r, c),
            device_id_type=MESH,
        )

    def spread_copy(buffer, sends, recvs, step, owner):
        return pltpu.make_async_remote_copy(
            src_ref=buffer.at[owner],
            dst_ref=buffer.at[owner],
            send_sem=sends.at[step],
            recv_sem=recvs.at[step],
            device_id=(other(step), r, c),
            device_id_type=MESH,
        )

    for step in FAR_FIRST:
        band_copy(step, o).start()
    bands[o] = corr[o]

    part_lane = lax.broadcasted_iota(jnp.int32, (8, T), 1)

    @pl.loop(0, SLOTS // 2)
    def _(pair):
        at = pl.ds(pl.multiple_of(pair * 16, 16), 16)
        below = pl.ds(pl.multiple_of(pair * 16 + T, 16), 16)
        row = [rows[pair * 2 + k] for k in range(2)]
        column = [cols[pair * 2 + k] for k in range(2)]
        for i in range(PROJ // 8):
            both = []
            for k in range(2):
                shift = lax.rem(T - column[k], T)
                parts = [pltpu.roll(win[j, pl.ds(row[k] + i * 8, 8)], shift, 1) for j in range(3)]
                keep = part_lane < T - column[k]
                both.append(
                    jnp.concatenate([jnp.where(keep, parts[j], parts[j + 1]) for j in range(2)], axis=1)
                )
            high, low = split(jnp.concatenate(both, axis=0))
            patches[at, pl.ds(i * PROJ, PROJ)] = high
            patches[below, pl.ds(i * PROJ, PROJ)] = low

    scores = lax.dot_general(
        patches[...], planes[...], (((1,), (1,)), ((), ())), preferred_element_type=F32
    )
    scores = (scores[:T, :T] + (scores[:T, T:] + scores[T:, :T])) + scores[T:, T:]
    at_row = lax.broadcasted_iota(jnp.int32, (T, T), 0)
    at_lane = lax.broadcasted_iota(jnp.int32, (T, T), 1)
    scores = jnp.where(at_row % 8 == at_lane % 8, scores, 0.0)
    scores = jnp.sum(scores.reshape(SLOTS, 8, T), axis=1)
    spread = jnp.sum(squares_v[...].T, axis=0, keepdims=True)
    for far in (4, 2, 1):
        scores = scores + pltpu.roll(scores, T - far, 1)
        spread = spread + pltpu.roll(spread, T - far, 1)
    scores = scores * ((1.0 / PROJ) / jnp.sqrt(spread * (1.0 / (PROJ * PROJ)) + 1e-6))
    lane = lax.broadcasted_iota(jnp.int32, (SLOTS, T), 1)
    local = jnp.max(jnp.where(lane % 8 == 0, scores, -jnp.inf), axis=1, keepdims=True)
    local = jnp.broadcast_to(local, (SLOTS, T))
    at_row = lax.broadcasted_iota(jnp.int32, (SLOTS, T), 0)
    at_lane = lax.broadcasted_iota(jnp.int32, (SLOTS, T), 1)
    local = jnp.sum(jnp.where(at_row == at_lane, local, 0.0), axis=0, keepdims=True)
    finals[o] = jnp.broadcast_to(local, (8, T))
    for step in FAR_FIRST:
        spread_copy(finals, final_send, final_recv, step, o).start()

    for step in FAR_FIRST:
        band_copy(step, other(-step)).wait_recv()
    best = bands[0]
    added = bands[0]
    squares = bands[0] * bands[0]
    for k in range(1, GROUP):
        value = bands[k]
        best = jnp.maximum(best, value)
        added = added + value
        squares = squares + value * value
    snr[o] = (best - added / GROUP) / jnp.sqrt(squares / GROUP + 1e-5)
    for step in FAR_FIRST:
        spread_copy(snr, snr_send, snr_recv, step, o).start()

    for step in FAR_FIRST:
        spread_copy(finals, final_send, final_recv, step, other(-step)).wait_recv()
    best_fine = finals[0]
    for k in range(1, GROUP):
        best_fine = jnp.maximum(best_fine, finals[k])
    best_out[...] = best_fine

    for step in FAR_FIRST:
        spread_copy(snr, snr_send, snr_recv, step, other(-step)).wait_recv()
    snr_out[...] = snr[...].reshape(T, T)

    for i, (dr, dc) in enumerate(NEAR):
        @pl.when(inside(dr, dc))
        def _():
            halo(i).wait_send()
    for step in FAR_FIRST:
        band_copy(step, o).wait_send()
        spread_copy(finals, final_send, final_recv, step, o).wait_send()
        spread_copy(snr, snr_send, snr_recv, step, o).wait_send()


def per_device(micrograph, templates, fine_templates, peak_rows, peak_cols, peak_count):
    consts = [jnp.asarray(x) for x in tables()]
    any_spec = pl.BlockSpec(memory_space=pl.ANY)
    smem = pl.BlockSpec(memory_space=pltpu.SMEM)
    vmem = pl.BlockSpec(memory_space=pltpu.VMEM)
    dma = pltpu.SemaphoreType.DMA
    regular = pltpu.SemaphoreType.REGULAR
    snr, best = pl.pallas_call(
        kernel,
        out_shape=(
            jax.ShapeDtypeStruct((T, T), F32),
            jax.ShapeDtypeStruct((8, T), F32),
        ),
        in_specs=[any_spec] * 3 + [smem] * 2 + [any_spec] * 5,
        out_specs=(vmem, vmem),
        scratch_shapes=[
            pltpu.VMEM((3, LEN, T), F32),
            pltpu.VMEM((PROJ, PROJ), F32),
            pltpu.VMEM((FINE, PROJ, PROJ), F32),
            pltpu.VMEM((2, 2 * T, 2 * T), BF16),
            pltpu.VMEM((2, T, T), BF16),
            pltpu.VMEM((2, 3, T, 2 * T), BF16),
            pltpu.VMEM((2, 3, T, 2 * T), BF16),
            pltpu.VMEM((2, LEN, T), BF16),
            pltpu.VMEM((3, T, LEN), F32),
            pltpu.VMEM((FINE, 8, T), F32),
            pltpu.VMEM((FINE * 8, T), F32),
            pltpu.VMEM((PROJ, PROJ * PROJ // 8), BF16),
            pltpu.VMEM((PROJ, PROJ * PROJ // 8), BF16),
            pltpu.VMEM((GROUP, 8, T), F32),
            pltpu.VMEM((GROUP, 8, T), F32),
            pltpu.VMEM((GROUP, 8, T), F32),
            pltpu.VMEM((GROUP, 8, T), F32),
            dma((8,)),
            dma((8,)),
            dma((8,)),
            dma((16,)),
            dma((16,)),
            dma((16,)),
            dma((16,)),
            dma((16,)),
            dma((16,)),
            regular,
            regular,
            regular,
        ],
        compiler_params=pltpu.CompilerParams(
            collective_id=0, has_side_effects=True
        ),
    )(micrograph, templates, fine_templates, peak_rows, peak_cols, *consts)
    slots = jnp.arange(SLOTS, dtype=jnp.int32)
    refined = jnp.where(slots < peak_count[0], best[0, :SLOTS], 0.0)
    return snr, refined


def solution(mesh):
    placed = (
        P("trow", "tcol"),
        P("orient", None, None),
        P("orient", None, None),
        P(("trow", "tcol")),
        P(("trow", "tcol")),
        P(("trow", "tcol")),
    )
    return jax.shard_map(
        per_device,
        mesh=mesh,
        in_specs=placed,
        out_specs=(P("trow", "tcol"), P(("trow", "tcol"))),
        check_vma=False,
    )
```

```python
import jax
import jax.numpy as jnp
import numpy as np
from jax import lax
from jax.experimental import pallas as pl
from jax.experimental.pallas import tpu as pltpu
from jax.sharding import PartitionSpec as P

F32 = jnp.float32
BF16 = jnp.bfloat16
MESH = pl.DeviceIdType.MESH
T = 128
LEN = 3 * T
PROJ = 2 * T
GROUP = 16
SLOTS = 16
BANDS = 8
BAND = T // BANDS
FINE = 16
HALF_ROOT3 = float(np.sqrt(3.0) / 2.0)
NEAR = [(dr, dc) for dr in (-1, 0, 1) for dc in (-1, 0, 1) if (dr, dc) != (0, 0)]
ALONG_Z = (4, 3, 5, 2, 6, 1, 7)
FAR_FIRST = (8, 7, 9, 6, 10, 5, 11, 4, 12, 3, 13, 1, 15, 2, 14)


def hi_lo(table):
    high = table.astype(BF16)
    low = (table - high.astype(np.float64)).astype(BF16)
    return high, low


def left_terms(table):
    high, low = hi_lo(table)
    return np.concatenate([high, low, high], axis=-1)


def right_terms(table):
    high, low = hi_lo(table)
    return np.concatenate([high, high, low], axis=0)


def tables():
    b = np.arange(T)
    q = np.arange(T)
    k0 = 3 * q + 0.5
    k1 = 3 * np.arange(T // 2) + 1.5
    unit = 2.0 * np.pi / LEN
    a0 = unit * np.outer(b, k0)
    a1 = unit * np.outer(b, k1)
    row0 = np.block([[np.cos(a0), -np.sin(a0)], [np.sin(a0), np.cos(a0)]])
    row1 = np.concatenate([np.cos(a1), -np.sin(a1)], 1)
    col, inv = [], []
    for r in range(3):
        th = unit * np.outer(3 * q + r, b)
        col.append(np.concatenate([np.cos(th), np.sin(th)], 1))
        inv.append(np.concatenate([np.cos(th).T, -np.sin(th).T], 1))
    back = np.concatenate([np.cos(a0).T, -np.sin(a0).T, np.cos(a1).T, -np.sin(a1).T], 0)
    back = back * (2.0 / (LEN * LEN * PROJ))
    return (
        right_terms(row0),
        right_terms(row1),
        left_terms(np.stack(col)),
        left_terms(np.stack(inv)),
        right_terms(back),
    )


def split(x):
    high = x.astype(BF16)
    return high, (x - high.astype(F32)).astype(BF16)


def dot(a, b):
    return jnp.dot(a, b, preferred_element_type=F32)


def table_times(table, x):
    high, low = split(x)
    return dot(table, jnp.concatenate([high, high, low], axis=0))


def times_table(x, table):
    high, low = split(x)
    return dot(jnp.concatenate([high, low, high], axis=1), table)


def rotated(z):
    last = z[:, 2 * T :]
    lane = lax.broadcasted_iota(jnp.int32, last.shape, 1)
    turned = pltpu.roll(last, T // 2, 1)
    turned = jnp.where(lane < T // 2, turned, -turned)
    return jnp.concatenate([z[:, T : 2 * T], -z[:, :T], turned], axis=1)


def with_rotated(z):
    return jnp.concatenate([z, rotated(z)], axis=0)


def kernel(
    tile, template, fine, rows_in, cols_in, row0, row1, col, inv, back,
    snr_out, best_out,
    win, tmpl, fine_v, row0_v, row1_v, col_v, inv_v, back_v, spec,
    sums, squares_v, patches, planes, corr, bands, snr, finals, rows, cols,
    load_sem, halo_send, halo_recv, band_send, band_recv,
    snr_send, snr_recv, final_send, final_recv, near_sem, mid_sem, far_sem,
):
    o = lax.axis_index("orient")
    r = lax.axis_index("trow")
    c = lax.axis_index("tcol")

    loads = [
        pltpu.make_async_copy(src, dst, load_sem.at[i])
        for i, (src, dst) in enumerate(
            [
                (template.at[0], tmpl),
                (row0, row0_v),
                (row1, row1_v),
                (col, col_v),
                (tile, win.at[1, pl.ds(T, T)]),
                (fine, fine_v),
                (inv, inv_v),
                (back, back_v),
                (rows_in, rows),
                (cols_in, cols),
            ]
        )
    ]
    for load in loads:
        load.start()

    def other(step):
        return lax.rem(o + (step % GROUP), GROUP)

    def inside(dr, dc):
        checks = []
        if dr < 0:
            checks.append(r > 0)
        if dr > 0:
            checks.append(r < 3)
        if dc < 0:
            checks.append(c > 0)
        if dc > 0:
            checks.append(c < 3)
        out = checks[0]
        for check in checks[1:]:
            out = jnp.logical_and(out, check)
        return out

    mate = o + 1 - 2 * lax.rem(o, 2)
    barrier = pltpu.get_barrier_semaphore()
    for dr, dc in NEAR:
        @pl.when(inside(dr, dc))
        def _():
            pl.semaphore_signal(barrier, inc=1, device_id=(o, r + dr, c + dc), device_id_type=MESH)
    for peer in (other(2), other(14), mate):
        pl.semaphore_signal(barrier, inc=1, device_id=(peer, r, c), device_id_type=MESH)
    across = 3 - (r == 0).astype(jnp.int32) - (r == 3).astype(jnp.int32)
    along = 3 - (c == 0).astype(jnp.int32) - (c == 3).astype(jnp.int32)
    pl.semaphore_wait(barrier, across * along + 2)

    def halo(i):
        dr, dc = NEAR[i]
        return pltpu.make_async_remote_copy(
            src_ref=tile,
            dst_ref=win.at[1 - dc, pl.ds((1 - dr) * T, T)],
            send_sem=halo_send.at[i],
            recv_sem=halo_recv.at[i],
            device_id=(o, r + dr, c + dc),
            device_id_type=MESH,
        )

    for i, (dr, dc) in enumerate(NEAR):
        @pl.when(inside(dr, dc))
        def _():
            halo(i).start()

        @pl.when(jnp.logical_not(inside(dr, dc)))
        def _():
            win[1 + dc, pl.ds((1 + dr) * T, T)] = jnp.zeros((T, T), F32)

    for peer in (other(2), other(14)):
        pl.semaphore_signal(near_sem, inc=1, device_id=(peer, r, c), device_id_type=MESH)

    def row_dft(x0, x1, x2):
        if x2 is None:
            mixed = jnp.concatenate([x0 + 0.5 * x1, -HALF_ROOT3 * x1], axis=1)
            real = x0 - x1
        else:
            mixed = jnp.concatenate([x0 + 0.5 * (x1 - x2), -HALF_ROOT3 * (x1 + x2)], axis=1)
            real = x0 - x1 + x2
        return jnp.concatenate(
            [times_table(mixed, row0_v[...]), times_table(real, row1_v[...])], axis=1
        )

    def col_dft(b0, b1, b2):
        if b2 is None:
            total = b0 + b1
            even = b0 - 0.5 * b1
            odd = rotated(HALF_ROOT3 * b1)
        else:
            total = b0 + (b1 + b2)
            even = b0 - 0.5 * (b1 + b2)
            odd = rotated(HALF_ROOT3 * (b1 - b2))
        for k, z in enumerate((total, even + odd, even - odd)):
            yield table_times(col_v[k], with_rotated(z))

    for load in loads[:4]:
        load.wait()
    t = tmpl[...]
    t = t - jnp.sum(t, keepdims=True) * (1.0 / (PROJ * PROJ))
    spread = jnp.sum(t * t, keepdims=True) * (1.0 / (PROJ * PROJ))
    t = t / jnp.sqrt(spread + 1e-6)
    t = row_dft(t[:, :T], t[:, T:], None)
    for k, z in enumerate(col_dft(t[:T], t[T:], None)):
        spec[k] = z

    loads[5].wait()

    @pl.loop(0, FINE)
    def _(f):
        part = jnp.sum(fine_v[f].reshape(PROJ // 8, 8, PROJ), axis=0)
        sums[f] = part[:, :T] + part[:, T:]

    mean = jnp.sum(sums[...], axis=(1, 2), keepdims=True) * (1.0 / (PROJ * PROJ))
    sums[...] = jnp.broadcast_to(mean, (FINE, 8, T))

    pl.semaphore_wait(near_sem, 2)
    for peer in (other(4), other(12)):
        pl.semaphore_signal(mid_sem, inc=1, device_id=(peer, r, c), device_id_type=MESH)

    @pl.loop(0, FINE // 2)
    def _(pair):
        at = pl.ds(pl.multiple_of(pair * 16, 16), 16)
        below = pl.ds(pl.multiple_of(pair * 16 + T, 16), 16)
        mean = jnp.concatenate([sums[pair * 2], sums[pair * 2 + 1]], axis=0)
        mean = jnp.concatenate([mean, mean], axis=1)
        total = jnp.zeros((16, PROJ), F32)
        for i in range(PROJ // 8):
            group = pl.ds(i * 8, 8)
            x = jnp.concatenate([fine_v[pair * 2, group], fine_v[pair * 2 + 1, group]], axis=0) - mean
            total = total + x * x
            high, low = split(x)
            planes[at, pl.ds(i * PROJ, PROJ)] = high
            planes[below, pl.ds(i * PROJ, PROJ)] = low
        squares_v[at] = total[:, :T] + total[:, T:]

    pl.semaphore_wait(mid_sem, 2)
    pl.semaphore_signal(far_sem, inc=1, device_id=(other(8), r, c), device_id_type=MESH)

    loads[4].wait()
    loads[6].wait()
    loads[7].wait()
    for i, (dr, dc) in enumerate(NEAR):
        @pl.when(inside(-dr, -dc))
        def _():
            halo(i).wait_recv()

    w = row_dft(win[0], win[1], win[2])
    total = jnp.zeros((T, LEN), F32)
    lane = lax.broadcasted_iota(jnp.int32, (T, T), 1)
    for k, z in enumerate(col_dft(w[:T], w[T : 2 * T], w[2 * T :])):
        s = spec[k]
        last = s[:, 2 * T :]
        turned = pltpu.roll(last, T // 2, 1)
        re = jnp.concatenate([s[:, :T], s[:, :T], jnp.where(lane < T // 2, last, turned)], axis=1)
        im = jnp.concatenate(
            [s[:, T : 2 * T], s[:, T : 2 * T], jnp.where(lane < T // 2, turned, last)], axis=1
        )
        prod = z * re + rotated(z) * im
        total = total + table_times(inv_v[k], with_rotated(prod))
    corr[...] = times_table(total, back_v[...]).reshape(BANDS, BAND, T)

    pl.semaphore_wait(far_sem, 1)

    def band_copy(step, owner):
        return pltpu.make_async_remote_copy(
            src_ref=corr.at[lax.div(other(step), 2)],
            dst_ref=bands.at[owner],
            send_sem=band_send.at[step],
            recv_sem=band_recv.at[step],
            device_id=(other(step), r, c),
            device_id_type=MESH,
        )

    def final_copy(step, owner):
        return pltpu.make_async_remote_copy(
            src_ref=finals.at[owner],
            dst_ref=finals.at[owner],
            send_sem=final_send.at[step],
            recv_sem=final_recv.at[step],
            device_id=(other(step), r, c),
            device_id_type=MESH,
        )

    def snr_copy(step, owner):
        return pltpu.make_async_remote_copy(
            src_ref=snr.at[owner],
            dst_ref=snr.at[owner],
            send_sem=snr_send.at[step],
            recv_sem=snr_recv.at[step],
            device_id=(other(2 * step), r, c),
            device_id_type=MESH,
        )

    for step in FAR_FIRST:
        band_copy(step, o).start()
    layer = lax.div(o, 2)
    bands[o] = corr[layer]

    loads[8].wait()
    loads[9].wait()
    part_lane = lax.broadcasted_iota(jnp.int32, (8, T), 1)

    @pl.loop(0, SLOTS // 2)
    def _(pair):
        at = pl.ds(pl.multiple_of(pair * 16, 16), 16)
        below = pl.ds(pl.multiple_of(pair * 16 + T, 16), 16)
        row = [rows[pair * 2 + k] for k in range(2)]
        column = [cols[pair * 2 + k] for k in range(2)]
        for i in range(PROJ // 8):
            both = []
            for k in range(2):
                shift = lax.rem(T - column[k], T)
                parts = [pltpu.roll(win[j, pl.ds(row[k] + i * 8, 8)], shift, 1) for j in range(3)]
                keep = part_lane < T - column[k]
                both.append(
                    jnp.concatenate([jnp.where(keep, parts[j], parts[j + 1]) for j in range(2)], axis=1)
                )
            high, low = split(jnp.concatenate(both, axis=0))
            patches[at, pl.ds(i * PROJ, PROJ)] = high
            patches[below, pl.ds(i * PROJ, PROJ)] = low

    scores = lax.dot_general(
        patches[...], planes[...], (((1,), (1,)), ((), ())), preferred_element_type=F32
    )
    scores = (scores[:T, :T] + (scores[:T, T:] + scores[T:, :T])) + scores[T:, T:]
    at_row = lax.broadcasted_iota(jnp.int32, (T, T), 0)
    at_lane = lax.broadcasted_iota(jnp.int32, (T, T), 1)
    scores = jnp.where(at_row % 8 == at_lane % 8, scores, 0.0)
    scores = jnp.sum(scores.reshape(SLOTS, 8, T), axis=1)
    spread = jnp.sum(squares_v[...].T, axis=0, keepdims=True)
    for far in (4, 2, 1):
        scores = scores + pltpu.roll(scores, T - far, 1)
        spread = spread + pltpu.roll(spread, T - far, 1)
    scores = scores * ((1.0 / PROJ) / jnp.sqrt(spread * (1.0 / (PROJ * PROJ)) + 1e-6))
    lane = lax.broadcasted_iota(jnp.int32, (SLOTS, T), 1)
    local = jnp.max(jnp.where(lane % 8 == 0, scores, -jnp.inf), axis=1, keepdims=True)
    local = jnp.broadcast_to(local, (SLOTS, T))
    at_row = lax.broadcasted_iota(jnp.int32, (SLOTS, T), 0)
    at_lane = lax.broadcasted_iota(jnp.int32, (SLOTS, T), 1)
    local = jnp.sum(jnp.where(at_row == at_lane, local, 0.0), axis=0, keepdims=True)
    finals[o] = jnp.broadcast_to(local, (8, T))
    for step in FAR_FIRST:
        final_copy(step, o).start()

    for step in FAR_FIRST:
        band_copy(step, other(-step)).wait_recv()
    best = bands[0]
    added = bands[0]
    squares = bands[0] * bands[0]
    for k in range(1, GROUP):
        value = bands[k]
        best = jnp.maximum(best, value)
        added = added + value
        squares = squares + value * value
    snr[layer] = (best - added / GROUP) / jnp.sqrt(squares / GROUP + 1e-5)
    for step in ALONG_Z:
        snr_copy(step, layer).start()

    for step in FAR_FIRST:
        final_copy(step, other(-step)).wait_recv()
    best_fine = finals[0]
    for k in range(1, GROUP):
        best_fine = jnp.maximum(best_fine, finals[k])
    best_out[...] = best_fine

    for step in ALONG_Z:
        snr_copy(step, lax.div(other(-2 * step), 2)).wait_recv()
    snr_out[...] = snr[...].reshape(T, T)

    for i, (dr, dc) in enumerate(NEAR):
        @pl.when(inside(dr, dc))
        def _():
            halo(i).wait_send()
    for step in FAR_FIRST:
        band_copy(step, o).wait_send()
        final_copy(step, o).wait_send()
    for step in ALONG_Z:
        snr_copy(step, layer).wait_send()


def per_device(micrograph, templates, fine_templates, peak_rows, peak_cols, peak_count):
    consts = [jnp.asarray(x) for x in tables()]
    any_spec = pl.BlockSpec(memory_space=pl.ANY)
    vmem = pl.BlockSpec(memory_space=pltpu.VMEM)
    dma = pltpu.SemaphoreType.DMA
    regular = pltpu.SemaphoreType.REGULAR
    snr, best = pl.pallas_call(
        kernel,
        out_shape=(
            jax.ShapeDtypeStruct((T, T), F32),
            jax.ShapeDtypeStruct((8, T), F32),
        ),
        in_specs=[any_spec] * 10,
        out_specs=(vmem, vmem),
        scratch_shapes=[
            pltpu.VMEM((3, LEN, T), F32),
            pltpu.VMEM((PROJ, PROJ), F32),
            pltpu.VMEM((FINE, PROJ, PROJ), F32),
            pltpu.VMEM((6 * T, 2 * T), BF16),
            pltpu.VMEM((3 * T, T), BF16),
            pltpu.VMEM((3, T, 6 * T), BF16),
            pltpu.VMEM((3, T, 6 * T), BF16),
            pltpu.VMEM((3 * LEN, T), BF16),
            pltpu.VMEM((3, T, LEN), F32),
            pltpu.VMEM((FINE, 8, T), F32),
            pltpu.VMEM((FINE * 8, T), F32),
            pltpu.VMEM((PROJ, PROJ * PROJ // 8), BF16),
            pltpu.VMEM((PROJ, PROJ * PROJ // 8), BF16),
            pltpu.VMEM((BANDS, BAND, T), F32),
            pltpu.VMEM((GROUP, BAND, T), F32),
            pltpu.VMEM((BANDS, BAND, T), F32),
            pltpu.VMEM((GROUP, 8, T), F32),
            pltpu.SMEM((SLOTS,), jnp.int32),
            pltpu.SMEM((SLOTS,), jnp.int32),
            dma((10,)),
            dma((8,)),
            dma((8,)),
            dma((16,)),
            dma((16,)),
            dma((16,)),
            dma((16,)),
            dma((16,)),
            dma((16,)),
            regular,
            regular,
            regular,
        ],
        compiler_params=pltpu.CompilerParams(
            collective_id=0, has_side_effects=True
        ),
    )(micrograph, templates, fine_templates, peak_rows, peak_cols, *consts)
    slots = jnp.arange(SLOTS, dtype=jnp.int32)
    refined = jnp.where(slots < peak_count[0], best[0, :SLOTS], 0.0)
    return snr, refined


def solution(mesh):
    placed = (
        P("trow", "tcol"),
        P("orient", None, None),
        P("orient", None, None),
        P(("trow", "tcol")),
        P(("trow", "tcol")),
        P(("trow", "tcol")),
    )
    return jax.shard_map(
        per_device,
        mesh=mesh,
        in_specs=placed,
        out_specs=(P("trow", "tcol"), P(("trow", "tcol"))),
        check_vma=False,
    )
```

```python
import jax
import jax.numpy as jnp
import numpy as np
from jax import lax
from jax.experimental import pallas as pl
from jax.experimental.pallas import tpu as pltpu
from jax.sharding import PartitionSpec as P

F32 = jnp.float32
BF16 = jnp.bfloat16
MESH = pl.DeviceIdType.MESH
T = 128
LEN = 3 * T
PROJ = 2 * T
GROUP = 16
SLOTS = 16
BANDS = 8
BAND = T // BANDS
FINE = 16
HALF_ROOT3 = float(np.sqrt(3.0) / 2.0)
NEAR = [(dr, dc) for dr in (-1, 0, 1) for dc in (-1, 0, 1) if (dr, dc) != (0, 0)]
ALONG_Z = (4, 3, 5, 2, 6, 1, 7)
FAR_FIRST = (8, 7, 9, 6, 10, 5, 11, 4, 12, 3, 13, 1, 15, 2, 14)


def hi_lo(table):
    high = table.astype(BF16)
    low = (table - high.astype(np.float64)).astype(BF16)
    return high, low


def side_by_side(table):
    return np.concatenate(hi_lo(table), axis=-1)


def stacked(table):
    return np.concatenate(hi_lo(table), axis=-2)


def tables():
    b = np.arange(T)
    k0 = 3 * b + 0.5
    k1 = 3 * np.arange(T // 2) + 1.5
    unit = 2.0 * np.pi / LEN
    a0 = unit * np.outer(k0, b)
    a1 = unit * np.outer(k1, b)
    first0 = np.block([[np.cos(a0), np.sin(a0)], [-np.sin(a0), np.cos(a0)]])
    first1 = np.concatenate([np.cos(a1), -np.sin(a1)], 0)
    second = []
    for r in range(3):
        cos, sin = np.cos(unit * np.outer(b, 3 * b + r)), np.sin(unit * np.outer(b, 3 * b + r))
        second.append(np.block([[cos, -sin], [sin, cos]]))
    second = np.stack(second)
    back = np.concatenate([np.cos(a0).T, np.cos(a1).T, -np.sin(a0).T, -np.sin(a1).T], 1)
    back = back * (2.0 / (LEN * LEN * PROJ))
    return (
        side_by_side(first0),
        side_by_side(first1),
        stacked(second),
        stacked(np.swapaxes(second, 1, 2)),
        side_by_side(back),
    )


def split(x):
    high = x.astype(BF16)
    return high, (x - high.astype(F32)).astype(BF16)


def dot(a, b):
    return jnp.dot(a, b, preferred_element_type=F32)


def table_times(table, x):
    high, low = split(x)
    depth = x.shape[0]
    table = jnp.concatenate([table, table[:, :depth]], axis=1)
    return dot(table, jnp.concatenate([high, high, low], axis=0))


def times_terms(x, table):
    high, low = split(x)
    depth = x.shape[1]
    return [high, low, high], [table[:depth], table]


def joined_dot(left, right):
    return dot(jnp.concatenate(left, axis=1), jnp.concatenate(right, axis=0))


def kernel(
    tile, template, fine, rows_in, cols_in, first0, first1, second, inv, back,
    snr_out, best_out,
    win, tmpl, fine_v, first0_v, first1_v, second_v, inv_v, back_v, spec,
    sums, squares_v, patches, planes, corr, bands, snr, finals, rows, cols,
    load_sem, halo_send, halo_recv, band_send, band_recv,
    snr_send, snr_recv, final_send, final_recv, near_sem, mid_sem, far_sem,
):
    o = lax.axis_index("orient")
    r = lax.axis_index("trow")
    c = lax.axis_index("tcol")

    loads = [
        pltpu.make_async_copy(src, dst, load_sem.at[i])
        for i, (src, dst) in enumerate(
            [
                (template.at[0], tmpl),
                (first0, first0_v),
                (first1, first1_v),
                (second, second_v),
                (tile, win.at[1, pl.ds(T, T)]),
                (fine, fine_v),
                (inv, inv_v),
                (back, back_v),
                (rows_in, rows),
                (cols_in, cols),
            ]
        )
    ]
    for load in loads:
        load.start()

    def other(step):
        return lax.rem(o + (step % GROUP), GROUP)

    def inside(dr, dc):
        checks = []
        if dr < 0:
            checks.append(r > 0)
        if dr > 0:
            checks.append(r < 3)
        if dc < 0:
            checks.append(c > 0)
        if dc > 0:
            checks.append(c < 3)
        out = checks[0]
        for check in checks[1:]:
            out = jnp.logical_and(out, check)
        return out

    mate = o + 1 - 2 * lax.rem(o, 2)
    barrier = pltpu.get_barrier_semaphore()
    for dr, dc in NEAR:
        @pl.when(inside(dr, dc))
        def _():
            pl.semaphore_signal(barrier, inc=1, device_id=(o, r + dr, c + dc), device_id_type=MESH)
    for peer in (other(2), other(14), mate):
        pl.semaphore_signal(barrier, inc=1, device_id=(peer, r, c), device_id_type=MESH)
    across = 3 - (r == 0).astype(jnp.int32) - (r == 3).astype(jnp.int32)
    along = 3 - (c == 0).astype(jnp.int32) - (c == 3).astype(jnp.int32)
    pl.semaphore_wait(barrier, across * along + 2)

    def halo(i):
        dr, dc = NEAR[i]
        return pltpu.make_async_remote_copy(
            src_ref=tile,
            dst_ref=win.at[1 - dc, pl.ds((1 - dr) * T, T)],
            send_sem=halo_send.at[i],
            recv_sem=halo_recv.at[i],
            device_id=(o, r + dr, c + dc),
            device_id_type=MESH,
        )

    for i, (dr, dc) in enumerate(NEAR):
        @pl.when(inside(dr, dc))
        def _():
            halo(i).start()

        @pl.when(jnp.logical_not(inside(dr, dc)))
        def _():
            win[1 + dc, pl.ds((1 + dr) * T, T)] = jnp.zeros((T, T), F32)

    for peer in (other(2), other(14)):
        pl.semaphore_signal(near_sem, inc=1, device_id=(peer, r, c), device_id_type=MESH)

    def first_pass(x0, x1, x2):
        if x2 is None:
            mixed = jnp.concatenate([x0 + 0.5 * x1, -HALF_ROOT3 * x1], axis=0)
            real = x0 - x1
        else:
            mixed = jnp.concatenate([x0 + 0.5 * (x1 - x2), -HALF_ROOT3 * (x1 + x2)], axis=0)
            real = x0 - x1 + x2
        a = table_times(first0_v[...], mixed)
        b = table_times(first1_v[...], real)
        return (
            jnp.concatenate([a[:T], b[: T // 2]], axis=0),
            jnp.concatenate([a[T:], b[T // 2 :]], axis=0),
        )

    def second_pass(re, im):
        r0, r1 = re[:, :T], re[:, T : 2 * T]
        i0, i1 = im[:, :T], im[:, T : 2 * T]
        if re.shape[1] == LEN:
            r2, i2 = re[:, 2 * T :], im[:, 2 * T :]
            ra, rb, ia, ib = r1 + r2, HALF_ROOT3 * (r1 - r2), i1 + i2, HALF_ROOT3 * (i1 - i2)
        else:
            ra, rb, ia, ib = r1, HALF_ROOT3 * r1, i1, HALF_ROOT3 * i1
        er, ei = r0 - 0.5 * ra, i0 - 0.5 * ia
        for k, pair in enumerate(((r0 + ra, i0 + ia), (er + ib, ei - rb), (er - ib, ei + rb))):
            yield joined_dot(*times_terms(jnp.concatenate(pair, axis=1), second_v[k]))

    for load in loads[:4]:
        load.wait()
    t = tmpl[...]
    t = t - jnp.sum(t, keepdims=True) * (1.0 / (PROJ * PROJ))
    spread = jnp.sum(t * t, keepdims=True) * (1.0 / (PROJ * PROJ))
    t = t / jnp.sqrt(spread + 1e-6)
    for k, z in enumerate(second_pass(*first_pass(t[:T], t[T:], None))):
        spec[k] = z

    loads[5].wait()

    @pl.loop(0, FINE)
    def _(f):
        part = jnp.sum(fine_v[f].reshape(PROJ // 8, 8, PROJ), axis=0)
        sums[f] = part[:, :T] + part[:, T:]

    mean = jnp.sum(sums[...], axis=(1, 2), keepdims=True) * (1.0 / (PROJ * PROJ))
    sums[...] = jnp.broadcast_to(mean, (FINE, 8, T))

    pl.semaphore_wait(near_sem, 2)
    for peer in (other(4), other(12)):
        pl.semaphore_signal(mid_sem, inc=1, device_id=(peer, r, c), device_id_type=MESH)

    @pl.loop(0, FINE // 2)
    def _(pair):
        at = pl.ds(pl.multiple_of(pair * 16, 16), 16)
        below = pl.ds(pl.multiple_of(pair * 16 + T, 16), 16)
        mean = jnp.concatenate([sums[pair * 2], sums[pair * 2 + 1]], axis=0)
        mean = jnp.concatenate([mean, mean], axis=1)
        total = jnp.zeros((16, PROJ), F32)
        for i in range(PROJ // 8):
            group = pl.ds(i * 8, 8)
            x = jnp.concatenate([fine_v[pair * 2, group], fine_v[pair * 2 + 1, group]], axis=0) - mean
            total = total + x * x
            high, low = split(x)
            planes[at, pl.ds(i * PROJ, PROJ)] = high
            planes[below, pl.ds(i * PROJ, PROJ)] = low
        squares_v[at] = total[:, :T] + total[:, T:]

    pl.semaphore_wait(mid_sem, 2)
    pl.semaphore_signal(far_sem, inc=1, device_id=(other(8), r, c), device_id_type=MESH)

    loads[4].wait()
    loads[6].wait()
    loads[7].wait()
    for i, (dr, dc) in enumerate(NEAR):
        @pl.when(inside(-dr, -dc))
        def _():
            halo(i).wait_recv()

    w = [
        jnp.concatenate([win[j, pl.ds(k * T, T)] for j in range(3)], axis=1) for k in range(3)
    ]
    left, right = [], []
    for k, z in enumerate(second_pass(*first_pass(*w))):
        wr, wi = z[:, :T], z[:, T:]
        tr, ti = spec[k, :, :T], spec[k, :, T:]
        prod = jnp.concatenate([wr * tr + wi * ti, wi * tr - wr * ti], axis=1)
        terms = times_terms(prod, inv_v[k])
        left += terms[0]
        right += terms[1]
    u = joined_dot(left, right)
    u = jnp.concatenate([u[:, :T], u[:, T:]], axis=0)
    corr[...] = table_times(back_v[...], u).reshape(BANDS, BAND, T)

    pl.semaphore_wait(far_sem, 1)

    def band_copy(step, owner):
        return pltpu.make_async_remote_copy(
            src_ref=corr.at[lax.div(other(step), 2)],
            dst_ref=bands.at[owner],
            send_sem=band_send.at[step],
            recv_sem=band_recv.at[step],
            device_id=(other(step), r, c),
            device_id_type=MESH,
        )

    def final_copy(step, owner):
        return pltpu.make_async_remote_copy(
            src_ref=finals.at[owner],
            dst_ref=finals.at[owner],
            send_sem=final_send.at[step],
            recv_sem=final_recv.at[step],
            device_id=(other(step), r, c),
            device_id_type=MESH,
        )

    def snr_copy(step, owner):
        return pltpu.make_async_remote_copy(
            src_ref=snr.at[owner],
            dst_ref=snr.at[owner],
            send_sem=snr_send.at[step],
            recv_sem=snr_recv.at[step],
            device_id=(other(2 * step), r, c),
            device_id_type=MESH,
        )

    for step in FAR_FIRST:
        band_copy(step, o).start()
    layer = lax.div(o, 2)
    bands[o] = corr[layer]

    loads[8].wait()
    loads[9].wait()
    part_lane = lax.broadcasted_iota(jnp.int32, (8, T), 1)

    @pl.loop(0, SLOTS // 2)
    def _(pair):
        at = pl.ds(pl.multiple_of(pair * 16, 16), 16)
        below = pl.ds(pl.multiple_of(pair * 16 + T, 16), 16)
        row = [rows[pair * 2 + k] for k in range(2)]
        column = [cols[pair * 2 + k] for k in range(2)]
        for i in range(PROJ // 8):
            both = []
            for k in range(2):
                shift = lax.rem(T - column[k], T)
                parts = [pltpu.roll(win[j, pl.ds(row[k] + i * 8, 8)], shift, 1) for j in range(3)]
                keep = part_lane < T - column[k]
                both.append(
                    jnp.concatenate([jnp.where(keep, parts[j], parts[j + 1]) for j in range(2)], axis=1)
                )
            high, low = split(jnp.concatenate(both, axis=0))
            patches[at, pl.ds(i * PROJ, PROJ)] = high
            patches[below, pl.ds(i * PROJ, PROJ)] = low

    scores = lax.dot_general(
        patches[...], planes[...], (((1,), (1,)), ((), ())), preferred_element_type=F32
    )
    scores = (scores[:T, :T] + (scores[:T, T:] + scores[T:, :T])) + scores[T:, T:]
    at_row = lax.broadcasted_iota(jnp.int32, (T, T), 0)
    at_lane = lax.broadcasted_iota(jnp.int32, (T, T), 1)
    scores = jnp.where(at_row % 8 == at_lane % 8, scores, 0.0)
    scores = jnp.sum(scores.reshape(SLOTS, 8, T), axis=1)
    spread = jnp.sum(squares_v[...].T, axis=0, keepdims=True)
    for far in (4, 2, 1):
        scores = scores + pltpu.roll(scores, T - far, 1)
        spread = spread + pltpu.roll(spread, T - far, 1)
    scores = scores * ((1.0 / PROJ) / jnp.sqrt(spread * (1.0 / (PROJ * PROJ)) + 1e-6))
    lane = lax.broadcasted_iota(jnp.int32, (SLOTS, T), 1)
    local = jnp.max(jnp.where(lane % 8 == 0, scores, -jnp.inf), axis=1, keepdims=True)
    local = jnp.broadcast_to(local, (SLOTS, T))
    at_row = lax.broadcasted_iota(jnp.int32, (SLOTS, T), 0)
    at_lane = lax.broadcasted_iota(jnp.int32, (SLOTS, T), 1)
    local = jnp.sum(jnp.where(at_row == at_lane, local, 0.0), axis=0, keepdims=True)
    finals[o] = jnp.broadcast_to(local, (8, T))
    for step in FAR_FIRST:
        final_copy(step, o).start()

    for step in FAR_FIRST:
        band_copy(step, other(-step)).wait_recv()
    best = bands[0]
    added = bands[0]
    squares = bands[0] * bands[0]
    for k in range(1, GROUP):
        value = bands[k]
        best = jnp.maximum(best, value)
        added = added + value
        squares = squares + value * value
    snr[layer] = (best - added / GROUP) / jnp.sqrt(squares / GROUP + 1e-5)
    for step in ALONG_Z:
        snr_copy(step, layer).start()

    for step in FAR_FIRST:
        final_copy(step, other(-step)).wait_recv()
    best_fine = finals[0]
    for k in range(1, GROUP):
        best_fine = jnp.maximum(best_fine, finals[k])
    best_out[...] = best_fine

    for step in ALONG_Z:
        snr_copy(step, lax.div(other(-2 * step), 2)).wait_recv()
    snr_out[...] = snr[...].reshape(T, T)

    for i, (dr, dc) in enumerate(NEAR):
        @pl.when(inside(dr, dc))
        def _():
            halo(i).wait_send()
    for step in FAR_FIRST:
        band_copy(step, o).wait_send()
        final_copy(step, o).wait_send()
    for step in ALONG_Z:
        snr_copy(step, layer).wait_send()


def per_device(micrograph, templates, fine_templates, peak_rows, peak_cols, peak_count):
    consts = [jnp.asarray(x) for x in tables()]
    any_spec = pl.BlockSpec(memory_space=pl.ANY)
    vmem = pl.BlockSpec(memory_space=pltpu.VMEM)
    dma = pltpu.SemaphoreType.DMA
    regular = pltpu.SemaphoreType.REGULAR
    snr, best = pl.pallas_call(
        kernel,
        out_shape=(
            jax.ShapeDtypeStruct((T, T), F32),
            jax.ShapeDtypeStruct((8, T), F32),
        ),
        in_specs=[any_spec] * 10,
        out_specs=(vmem, vmem),
        scratch_shapes=[
            pltpu.VMEM((3, LEN, T), F32),
            pltpu.VMEM((PROJ, PROJ), F32),
            pltpu.VMEM((FINE, PROJ, PROJ), F32),
            pltpu.VMEM((2 * T, 4 * T), BF16),
            pltpu.VMEM((T, 2 * T), BF16),
            pltpu.VMEM((3, 4 * T, 2 * T), BF16),
            pltpu.VMEM((3, 4 * T, 2 * T), BF16),
            pltpu.VMEM((T, 2 * LEN), BF16),
            pltpu.VMEM((3, LEN // 2, 2 * T), F32),
            pltpu.VMEM((FINE, 8, T), F32),
            pltpu.VMEM((FINE * 8, T), F32),
            pltpu.VMEM((PROJ, PROJ * PROJ // 8), BF16),
            pltpu.VMEM((PROJ, PROJ * PROJ // 8), BF16),
            pltpu.VMEM((BANDS, BAND, T), F32),
            pltpu.VMEM((GROUP, BAND, T), F32),
            pltpu.VMEM((BANDS, BAND, T), F32),
            pltpu.VMEM((GROUP, 8, T), F32),
            pltpu.SMEM((SLOTS,), jnp.int32),
            pltpu.SMEM((SLOTS,), jnp.int32),
            dma((10,)),
            dma((8,)),
            dma((8,)),
            dma((16,)),
            dma((16,)),
            dma((16,)),
            dma((16,)),
            dma((16,)),
            dma((16,)),
            regular,
            regular,
            regular,
        ],
        compiler_params=pltpu.CompilerParams(
            collective_id=0, has_side_effects=True
        ),
    )(micrograph, templates, fine_templates, peak_rows, peak_cols, *consts)
    slots = jnp.arange(SLOTS, dtype=jnp.int32)
    refined = jnp.where(slots < peak_count[0], best[0, :SLOTS], 0.0)
    return snr, refined


def solution(mesh):
    placed = (
        P("trow", "tcol"),
        P("orient", None, None),
        P("orient", None, None),
        P(("trow", "tcol")),
        P(("trow", "tcol")),
        P(("trow", "tcol")),
    )
    return jax.shard_map(
        per_device,
        mesh=mesh,
        in_specs=placed,
        out_specs=(P("trow", "tcol"), P(("trow", "tcol"))),
        check_vma=False,
    )
```

```python
import jax
import jax.numpy as jnp
import numpy as np
from jax import lax
from jax.experimental import pallas as pl
from jax.experimental.pallas import tpu as pltpu
from jax.sharding import PartitionSpec as P

F32 = jnp.float32
BF16 = jnp.bfloat16
MESH = pl.DeviceIdType.MESH
T = 128
LEN = 3 * T
PROJ = 2 * T
GROUP = 16
SLOTS = 16
BANDS = 8
BAND = T // BANDS
FINE = 16
HALF_ROOT3 = float(np.sqrt(3.0) / 2.0)
NEAR = [(dr, dc) for dr in (-1, 0, 1) for dc in (-1, 0, 1) if (dr, dc) != (0, 0)]
ALONG_Z = (4, 3, 5, 2, 6, 1, 7)
FAR_FIRST = (8, 7, 9, 6, 10, 5, 11, 4, 12, 3, 13, 1, 15, 2, 14)


def hi_lo(table):
    high = table.astype(BF16)
    low = (table - high.astype(np.float64)).astype(BF16)
    return high, low


def side_by_side(table):
    return np.concatenate(hi_lo(table), axis=-1)


def stacked(table):
    return np.concatenate(hi_lo(table), axis=-2)


def tables():
    b = np.arange(T)
    k0 = 3 * b + 0.5
    k1 = 3 * np.arange(T // 2) + 1.5
    unit = 2.0 * np.pi / LEN
    a0 = unit * np.outer(k0, b)
    a1 = unit * np.outer(k1, b)
    first0 = np.block([[np.cos(a0), np.sin(a0)], [-np.sin(a0), np.cos(a0)]])
    first1 = np.concatenate([np.cos(a1), -np.sin(a1)], 0)
    second = []
    for r in range(3):
        cos, sin = np.cos(unit * np.outer(b, 3 * b + r)), np.sin(unit * np.outer(b, 3 * b + r))
        second.append(np.block([[cos, -sin], [sin, cos]]))
    second = np.stack(second)
    back = np.concatenate([np.cos(a0).T, np.cos(a1).T, -np.sin(a0).T, -np.sin(a1).T], 1)
    back = back * (2.0 / (LEN * LEN * PROJ))
    return (
        side_by_side(first0),
        side_by_side(first1),
        stacked(second),
        stacked(np.swapaxes(second, 1, 2)),
        side_by_side(back),
    )


def split(x):
    high = x.astype(BF16)
    return high, (x - high.astype(F32)).astype(BF16)


def dot(a, b):
    return jnp.dot(a, b, preferred_element_type=F32)


def table_times(table, x):
    high, low = split(x)
    depth = x.shape[0]
    table = jnp.concatenate([table, table[:, :depth]], axis=1)
    return dot(table, jnp.concatenate([high, high, low], axis=0))


def times_terms(x, table):
    high, low = split(x)
    depth = x.shape[1]
    return [high, low, high], [table[:depth], table]


def joined_dot(left, right):
    return dot(jnp.concatenate(left, axis=1), jnp.concatenate(right, axis=0))


def kernel(
    tile, template, fine, rows_in, cols_in, count_in, first0, first1, second, inv, back,
    snr_out, best_out,
    win, tmpl, fine_v, first0_v, first1_v, second_v, inv_v, back_v, spec,
    sums, squares_v, patches, planes, corr, bands, snr, finals, rows, cols, count,
    load_sem, halo_send, halo_recv, band_send, band_recv,
    snr_send, snr_recv, final_send, final_recv, near_sem, mate_sem,
):
    o = lax.axis_index("orient")
    r = lax.axis_index("trow")
    c = lax.axis_index("tcol")

    loads = [
        pltpu.make_async_copy(src, dst, load_sem.at[i])
        for i, (src, dst) in enumerate(
            [
                (template.at[0], tmpl),
                (first0, first0_v),
                (first1, first1_v),
                (second, second_v),
                (tile, win.at[1, pl.ds(T, T)]),
                (fine, fine_v),
                (inv, inv_v),
                (back, back_v),
                (rows_in, rows),
                (cols_in, cols),
                (count_in, count),
            ]
        )
    ]
    for load in loads:
        load.start()

    def other(step):
        return lax.rem(o + (step % GROUP), GROUP)

    def inside(dr, dc):
        checks = []
        if dr < 0:
            checks.append(r > 0)
        if dr > 0:
            checks.append(r < 3)
        if dc < 0:
            checks.append(c > 0)
        if dc > 0:
            checks.append(c < 3)
        out = checks[0]
        for check in checks[1:]:
            out = jnp.logical_and(out, check)
        return out

    mate = o + 1 - 2 * lax.rem(o, 2)
    barrier = pltpu.get_barrier_semaphore()
    for dr, dc in NEAR:
        @pl.when(inside(dr, dc))
        def _():
            pl.semaphore_signal(barrier, inc=1, device_id=(o, r + dr, c + dc), device_id_type=MESH)
    for peer in (other(2), other(14), other(4), other(12), mate):
        pl.semaphore_signal(barrier, inc=1, device_id=(peer, r, c), device_id_type=MESH)
    across = 3 - (r == 0).astype(jnp.int32) - (r == 3).astype(jnp.int32)
    along = 3 - (c == 0).astype(jnp.int32) - (c == 3).astype(jnp.int32)
    pl.semaphore_wait(barrier, across * along + 4)

    def halo(i):
        dr, dc = NEAR[i]
        return pltpu.make_async_remote_copy(
            src_ref=tile,
            dst_ref=win.at[1 - dc, pl.ds((1 - dr) * T, T)],
            send_sem=halo_send.at[i],
            recv_sem=halo_recv.at[i],
            device_id=(o, r + dr, c + dc),
            device_id_type=MESH,
        )

    for i, (dr, dc) in enumerate(NEAR):
        @pl.when(inside(dr, dc))
        def _():
            halo(i).start()

        @pl.when(jnp.logical_not(inside(dr, dc)))
        def _():
            win[1 + dc, pl.ds((1 + dr) * T, T)] = jnp.zeros((T, T), F32)

    for peer in (other(4), other(12)):
        pl.semaphore_signal(near_sem, inc=1, device_id=(peer, r, c), device_id_type=MESH)

    def first_pass(x0, x1, x2):
        if x2 is None:
            mixed = jnp.concatenate([x0 + 0.5 * x1, -HALF_ROOT3 * x1], axis=0)
            real = x0 - x1
        else:
            mixed = jnp.concatenate([x0 + 0.5 * (x1 - x2), -HALF_ROOT3 * (x1 + x2)], axis=0)
            real = x0 - x1 + x2
        a = table_times(first0_v[...], mixed)
        b = table_times(first1_v[...], real)
        return (
            jnp.concatenate([a[:T], b[: T // 2]], axis=0),
            jnp.concatenate([a[T:], b[T // 2 :]], axis=0),
        )

    def second_pass(re, im):
        r0, r1 = re[:, :T], re[:, T : 2 * T]
        i0, i1 = im[:, :T], im[:, T : 2 * T]
        if re.shape[1] == LEN:
            r2, i2 = re[:, 2 * T :], im[:, 2 * T :]
            ra, rb, ia, ib = r1 + r2, HALF_ROOT3 * (r1 - r2), i1 + i2, HALF_ROOT3 * (i1 - i2)
        else:
            ra, rb, ia, ib = r1, HALF_ROOT3 * r1, i1, HALF_ROOT3 * i1
        er, ei = r0 - 0.5 * ra, i0 - 0.5 * ia
        for k, pair in enumerate(((r0 + ra, i0 + ia), (er + ib, ei - rb), (er - ib, ei + rb))):
            yield joined_dot(*times_terms(jnp.concatenate(pair, axis=1), second_v[k]))

    for load in loads[:4]:
        load.wait()
    t = tmpl[...]
    t = t - jnp.sum(t, keepdims=True) * (1.0 / (PROJ * PROJ))
    spread = jnp.sum(t * t, keepdims=True) * (1.0 / (PROJ * PROJ))
    t = t / jnp.sqrt(spread + 1e-6)
    for k, z in enumerate(second_pass(*first_pass(t[:T], t[T:], None))):
        spec[k] = z

    loads[5].wait()

    @pl.loop(0, FINE)
    def _(f):
        part = jnp.sum(fine_v[f].reshape(PROJ // 8, 8, PROJ), axis=0)
        sums[f] = part[:, :T] + part[:, T:]

    mean = jnp.sum(sums[...], axis=(1, 2), keepdims=True) * (1.0 / (PROJ * PROJ))
    sums[...] = jnp.broadcast_to(mean, (FINE, 8, T))

    pl.semaphore_wait(near_sem, 2)
    pl.semaphore_signal(mate_sem, inc=1, device_id=(mate, r, c), device_id_type=MESH)

    @pl.loop(0, FINE // 2)
    def _(pair):
        at = pl.ds(pl.multiple_of(pair * 16, 16), 16)
        below = pl.ds(pl.multiple_of(pair * 16 + T, 16), 16)
        mean = jnp.concatenate([sums[pair * 2], sums[pair * 2 + 1]], axis=0)
        mean = jnp.concatenate([mean, mean], axis=1)
        total = jnp.zeros((16, PROJ), F32)
        for i in range(PROJ // 8):
            group = pl.ds(i * 8, 8)
            x = jnp.concatenate([fine_v[pair * 2, group], fine_v[pair * 2 + 1, group]], axis=0) - mean
            total = total + x * x
            high, low = split(x)
            planes[at, pl.ds(i * PROJ, PROJ)] = high
            planes[below, pl.ds(i * PROJ, PROJ)] = low
        squares_v[at] = total[:, :T] + total[:, T:]

    pl.semaphore_wait(mate_sem, 1)

    loads[4].wait()
    loads[6].wait()
    loads[7].wait()
    for i, (dr, dc) in enumerate(NEAR):
        @pl.when(inside(-dr, -dc))
        def _():
            halo(i).wait_recv()

    w = [
        jnp.concatenate([win[j, pl.ds(k * T, T)] for j in range(3)], axis=1) for k in range(3)
    ]
    left, right = [], []
    for k, z in enumerate(second_pass(*first_pass(*w))):
        wr, wi = z[:, :T], z[:, T:]
        tr, ti = spec[k, :, :T], spec[k, :, T:]
        prod = jnp.concatenate([wr * tr + wi * ti, wi * tr - wr * ti], axis=1)
        terms = times_terms(prod, inv_v[k])
        left += terms[0]
        right += terms[1]
    u = joined_dot(left, right)
    u = jnp.concatenate([u[:, :T], u[:, T:]], axis=0)
    corr[...] = table_times(back_v[...], u).reshape(BANDS, BAND, T)

    def band_copy(step, owner):
        return pltpu.make_async_remote_copy(
            src_ref=corr.at[lax.div(other(step), 2)],
            dst_ref=bands.at[owner],
            send_sem=band_send.at[step],
            recv_sem=band_recv.at[step],
            device_id=(other(step), r, c),
            device_id_type=MESH,
        )

    def final_copy(step, owner):
        return pltpu.make_async_remote_copy(
            src_ref=finals.at[owner],
            dst_ref=finals.at[owner],
            send_sem=final_send.at[step],
            recv_sem=final_recv.at[step],
            device_id=(other(step), r, c),
            device_id_type=MESH,
        )

    def snr_copy(step, owner):
        return pltpu.make_async_remote_copy(
            src_ref=snr.at[owner],
            dst_ref=snr.at[owner],
            send_sem=snr_send.at[step],
            recv_sem=snr_recv.at[step],
            device_id=(other(2 * step), r, c),
            device_id_type=MESH,
        )

    for step in FAR_FIRST:
        band_copy(step, o).start()
    layer = lax.div(o, 2)
    bands[o] = corr[layer]

    loads[8].wait()
    loads[9].wait()
    part_lane = lax.broadcasted_iota(jnp.int32, (8, T), 1)

    @pl.loop(0, SLOTS // 2)
    def _(pair):
        at = pl.ds(pl.multiple_of(pair * 16, 16), 16)
        below = pl.ds(pl.multiple_of(pair * 16 + T, 16), 16)
        row = [rows[pair * 2 + k] for k in range(2)]
        column = [cols[pair * 2 + k] for k in range(2)]
        for i in range(PROJ // 8):
            both = []
            for k in range(2):
                shift = lax.rem(T - column[k], T)
                parts = [pltpu.roll(win[j, pl.ds(row[k] + i * 8, 8)], shift, 1) for j in range(3)]
                keep = part_lane < T - column[k]
                both.append(
                    jnp.concatenate([jnp.where(keep, parts[j], parts[j + 1]) for j in range(2)], axis=1)
                )
            high, low = split(jnp.concatenate(both, axis=0))
            patches[at, pl.ds(i * PROJ, PROJ)] = high
            patches[below, pl.ds(i * PROJ, PROJ)] = low

    scores = lax.dot_general(
        patches[...], planes[...], (((1,), (1,)), ((), ())), preferred_element_type=F32
    )
    scores = (scores[:T, :T] + (scores[:T, T:] + scores[T:, :T])) + scores[T:, T:]
    at_row = lax.broadcasted_iota(jnp.int32, (T, T), 0)
    at_lane = lax.broadcasted_iota(jnp.int32, (T, T), 1)
    scores = jnp.where(at_row % 8 == at_lane % 8, scores, 0.0)
    scores = jnp.sum(scores.reshape(SLOTS, 8, T), axis=1)
    spread = jnp.sum(squares_v[...].T, axis=0, keepdims=True)
    for far in (4, 2, 1):
        scores = scores + pltpu.roll(scores, T - far, 1)
        spread = spread + pltpu.roll(spread, T - far, 1)
    scores = scores * ((1.0 / PROJ) / jnp.sqrt(spread * (1.0 / (PROJ * PROJ)) + 1e-6))
    lane = lax.broadcasted_iota(jnp.int32, (SLOTS, T), 1)
    local = jnp.max(jnp.where(lane % 8 == 0, scores, -jnp.inf), axis=1, keepdims=True)
    local = jnp.broadcast_to(local, (SLOTS, T))
    at_row = lax.broadcasted_iota(jnp.int32, (SLOTS, T), 0)
    at_lane = lax.broadcasted_iota(jnp.int32, (SLOTS, T), 1)
    local = jnp.sum(jnp.where(at_row == at_lane, local, 0.0), axis=0, keepdims=True)
    finals[o] = jnp.broadcast_to(local, (8, T))
    for step in FAR_FIRST:
        final_copy(step, o).start()

    for step in FAR_FIRST:
        band_copy(step, other(-step)).wait_recv()
    best = bands[0]
    added = bands[0]
    squares = bands[0] * bands[0]
    for k in range(1, GROUP):
        value = bands[k]
        best = jnp.maximum(best, value)
        added = added + value
        squares = squares + value * value
    snr[layer] = (best - added / GROUP) / jnp.sqrt(squares / GROUP + 1e-5)
    for step in ALONG_Z:
        snr_copy(step, layer).start()

    for step in FAR_FIRST:
        final_copy(step, other(-step)).wait_recv()
    best_fine = finals[0]
    for k in range(1, GROUP):
        best_fine = jnp.maximum(best_fine, finals[k])
    loads[10].wait()
    slot = lax.broadcasted_iota(jnp.int32, (8, T), 1)
    best_out[...] = jnp.where(slot < count[0], best_fine, 0.0)

    for step in ALONG_Z:
        snr_copy(step, lax.div(other(-2 * step), 2)).wait_recv()
    snr_out[...] = snr[...].reshape(T, T)

    for i, (dr, dc) in enumerate(NEAR):
        @pl.when(inside(dr, dc))
        def _():
            halo(i).wait_send()
    for step in FAR_FIRST:
        band_copy(step, o).wait_send()
        final_copy(step, o).wait_send()
    for step in ALONG_Z:
        snr_copy(step, layer).wait_send()


def in_hbm(x):
    return pltpu.with_memory_space_constraint(x, pltpu.HBM)


def finish(snr, best, snr_out, refined):
    snr_out[...] = snr[...]
    refined[...] = best[0, :SLOTS]


def per_device(micrograph, templates, fine_templates, peak_rows, peak_cols, peak_count):
    consts = [in_hbm(jnp.asarray(x)) for x in tables()]
    arrays = [in_hbm(x) for x in (micrograph, templates, fine_templates, peak_rows, peak_cols)]
    any_spec = pl.BlockSpec(memory_space=pl.ANY)
    vmem = pl.BlockSpec(memory_space=pltpu.VMEM)
    dma = pltpu.SemaphoreType.DMA
    regular = pltpu.SemaphoreType.REGULAR
    snr, best = pl.pallas_call(
        kernel,
        out_shape=(
            jax.ShapeDtypeStruct((T, T), F32),
            jax.ShapeDtypeStruct((8, T), F32),
        ),
        in_specs=[any_spec] * 11,
        out_specs=(vmem, vmem),
        scratch_shapes=[
            pltpu.VMEM((3, LEN, T), F32),
            pltpu.VMEM((PROJ, PROJ), F32),
            pltpu.VMEM((FINE, PROJ, PROJ), F32),
            pltpu.VMEM((2 * T, 4 * T), BF16),
            pltpu.VMEM((T, 2 * T), BF16),
            pltpu.VMEM((3, 4 * T, 2 * T), BF16),
            pltpu.VMEM((3, 4 * T, 2 * T), BF16),
            pltpu.VMEM((T, 2 * LEN), BF16),
            pltpu.VMEM((3, LEN // 2, 2 * T), F32),
            pltpu.VMEM((FINE, 8, T), F32),
            pltpu.VMEM((FINE * 8, T), F32),
            pltpu.VMEM((PROJ, PROJ * PROJ // 8), BF16),
            pltpu.VMEM((PROJ, PROJ * PROJ // 8), BF16),
            pltpu.VMEM((BANDS, BAND, T), F32),
            pltpu.VMEM((GROUP, BAND, T), F32),
            pltpu.VMEM((BANDS, BAND, T), F32),
            pltpu.VMEM((GROUP, 8, T), F32),
            pltpu.SMEM((SLOTS,), jnp.int32),
            pltpu.SMEM((SLOTS,), jnp.int32),
            pltpu.SMEM((1,), jnp.int32),
            dma((11,)),
            dma((8,)),
            dma((8,)),
            dma((16,)),
            dma((16,)),
            dma((16,)),
            dma((16,)),
            dma((16,)),
            dma((16,)),
            regular,
            regular,
        ],
        compiler_params=pltpu.CompilerParams(
            collective_id=0, has_side_effects=True, vmem_limit_bytes=48 * 1024 * 1024
        ),
    )(*arrays, peak_count, *consts)
    return pl.pallas_call(
        finish,
        out_shape=(jax.ShapeDtypeStruct((T, T), F32), jax.ShapeDtypeStruct((SLOTS,), F32)),
        in_specs=[vmem, vmem],
        out_specs=(vmem, vmem),
        compiler_params=pltpu.CompilerParams(vmem_limit_bytes=1024 * 1024),
    )(snr, best)


def solution(mesh):
    placed = (
        P("trow", "tcol"),
        P("orient", None, None),
        P("orient", None, None),
        P(("trow", "tcol")),
        P(("trow", "tcol")),
        P(("trow", "tcol")),
    )
    return jax.shard_map(
        per_device,
        mesh=mesh,
        in_specs=placed,
        out_specs=(P("trow", "tcol"), P(("trow", "tcol"))),
        check_vma=False,
    )
```

```python
import jax
import jax.numpy as jnp
import numpy as np
from jax import lax
from jax.experimental import pallas as pl
from jax.experimental.pallas import tpu as pltpu
from jax.sharding import PartitionSpec as P

F32 = jnp.float32
BF16 = jnp.bfloat16
MESH = pl.DeviceIdType.MESH
T = 128
LEN = 3 * T
PROJ = 2 * T
GROUP = 16
SLOTS = 16
BANDS = 8
BAND = T // BANDS
FINE = 16
HALF_ROOT3 = float(np.sqrt(3.0) / 2.0)
NEAR = [(dr, dc) for dr in (-1, 0, 1) for dc in (-1, 0, 1) if (dr, dc) != (0, 0)]
ALONG_Z = (4, 3, 5, 2, 6, 1, 7)
FAR_FIRST = (8, 7, 9, 6, 10, 5, 11, 4, 12, 3, 13, 1, 15, 2, 14)


def hi_lo(table):
    high = table.astype(BF16)
    low = (table - high.astype(np.float64)).astype(BF16)
    return high, low


def side_by_side(table):
    return np.concatenate(hi_lo(table), axis=-1)


def stacked(table):
    return np.concatenate(hi_lo(table), axis=-2)


def tables():
    b = np.arange(T)
    k0 = 3 * b + 0.5
    k1 = 3 * np.arange(T // 2) + 1.5
    unit = 2.0 * np.pi / LEN
    a0 = unit * np.outer(k0, b)
    a1 = unit * np.outer(k1, b)
    first0 = np.block([[np.cos(a0), np.sin(a0)], [-np.sin(a0), np.cos(a0)]])
    first1 = np.concatenate([np.cos(a1), -np.sin(a1)], 0)
    second = []
    for r in range(3):
        cos, sin = np.cos(unit * np.outer(b, 3 * b + r)), np.sin(unit * np.outer(b, 3 * b + r))
        second.append(np.block([[cos, -sin], [sin, cos]]))
    second = np.stack(second)
    back = np.concatenate([np.cos(a0).T, np.cos(a1).T, -np.sin(a0).T, -np.sin(a1).T], 1)
    back = back * (2.0 / (LEN * LEN * PROJ))
    return (
        side_by_side(first0),
        side_by_side(first1),
        stacked(second),
        stacked(np.swapaxes(second, 1, 2)),
        side_by_side(back),
    )


def split(x):
    high = x.astype(BF16)
    return high, (x - high.astype(F32)).astype(BF16)


def dot(a, b):
    return jnp.dot(a, b, preferred_element_type=F32)


def table_times(table, x):
    high, low = split(x)
    depth = x.shape[0]
    table = jnp.concatenate([table, table[:, :depth]], axis=1)
    return dot(table, jnp.concatenate([high, high, low], axis=0))


def times_terms(x, table):
    high, low = split(x)
    depth = x.shape[1]
    return [high, low, high], [table[:depth], table]


def joined_dot(left, right):
    return dot(jnp.concatenate(left, axis=1), jnp.concatenate(right, axis=0))


def kernel(
    tile, template, fine, rows_in, cols_in, count_in, first0, first1, second, inv, back,
    snr_out, best_out,
    win, tmpl, fine_v, first0_v, first1_v, second_v, inv_v, back_v, spec,
    sums, squares_v, patches, planes, corr, bands, snr, finals, rows, cols, count,
    load_sem, halo_send, halo_recv, band_send, band_recv,
    snr_send, snr_recv, final_send, final_recv, near_sem, mid_sem, mate_sem,
):
    o = lax.axis_index("orient")
    r = lax.axis_index("trow")
    c = lax.axis_index("tcol")

    loads = [
        pltpu.make_async_copy(src, dst, load_sem.at[i])
        for i, (src, dst) in enumerate(
            [
                (template.at[0], tmpl),
                (first0, first0_v),
                (first1, first1_v),
                (second, second_v),
                (tile, win.at[1, pl.ds(T, T)]),
                (fine, fine_v),
                (inv, inv_v),
                (back, back_v),
                (rows_in, rows),
                (cols_in, cols),
                (count_in, count),
            ]
        )
    ]

    def other(step):
        return lax.rem(o + (step % GROUP), GROUP)

    def inside(dr, dc):
        checks = []
        if dr < 0:
            checks.append(r > 0)
        if dr > 0:
            checks.append(r < 3)
        if dc < 0:
            checks.append(c > 0)
        if dc > 0:
            checks.append(c < 3)
        out = checks[0]
        for check in checks[1:]:
            out = jnp.logical_and(out, check)
        return out

    mate = o + 1 - 2 * lax.rem(o, 2)
    barrier = pltpu.get_barrier_semaphore()
    for dr, dc in NEAR:
        @pl.when(inside(dr, dc))
        def _():
            pl.semaphore_signal(barrier, inc=1, device_id=(o, r + dr, c + dc), device_id_type=MESH)
    for peer in (other(2), other(14), mate):
        pl.semaphore_signal(barrier, inc=1, device_id=(peer, r, c), device_id_type=MESH)
    for load in loads:
        load.start()
    across = 3 - (r == 0).astype(jnp.int32) - (r == 3).astype(jnp.int32)
    along = 3 - (c == 0).astype(jnp.int32) - (c == 3).astype(jnp.int32)
    pl.semaphore_wait(barrier, across * along + 2)

    def halo(i):
        dr, dc = NEAR[i]
        return pltpu.make_async_remote_copy(
            src_ref=tile,
            dst_ref=win.at[1 - dc, pl.ds((1 - dr) * T, T)],
            send_sem=halo_send.at[i],
            recv_sem=halo_recv.at[i],
            device_id=(o, r + dr, c + dc),
            device_id_type=MESH,
        )

    for i, (dr, dc) in enumerate(NEAR):
        @pl.when(inside(dr, dc))
        def _():
            halo(i).start()

        @pl.when(jnp.logical_not(inside(dr, dc)))
        def _():
            win[1 + dc, pl.ds((1 + dr) * T, T)] = jnp.zeros((T, T), F32)

    for peer in (other(2), other(14)):
        pl.semaphore_signal(near_sem, inc=1, device_id=(peer, r, c), device_id_type=MESH)

    def first_pass(x0, x1, x2):
        if x2 is None:
            mixed = jnp.concatenate([x0 + 0.5 * x1, -HALF_ROOT3 * x1], axis=0)
            real = x0 - x1
        else:
            mixed = jnp.concatenate([x0 + 0.5 * (x1 - x2), -HALF_ROOT3 * (x1 + x2)], axis=0)
            real = x0 - x1 + x2
        a = table_times(first0_v[...], mixed)
        b = table_times(first1_v[...], real)
        return (
            jnp.concatenate([a[:T], b[: T // 2]], axis=0),
            jnp.concatenate([a[T:], b[T // 2 :]], axis=0),
        )

    def second_pass(re, im):
        r0, r1 = re[:, :T], re[:, T : 2 * T]
        i0, i1 = im[:, :T], im[:, T : 2 * T]
        if re.shape[1] == LEN:
            r2, i2 = re[:, 2 * T :], im[:, 2 * T :]
            ra, rb, ia, ib = r1 + r2, HALF_ROOT3 * (r1 - r2), i1 + i2, HALF_ROOT3 * (i1 - i2)
        else:
            ra, rb, ia, ib = r1, HALF_ROOT3 * r1, i1, HALF_ROOT3 * i1
        er, ei = r0 - 0.5 * ra, i0 - 0.5 * ia
        for k, pair in enumerate(((r0 + ra, i0 + ia), (er + ib, ei - rb), (er - ib, ei + rb))):
            yield joined_dot(*times_terms(jnp.concatenate(pair, axis=1), second_v[k]))

    for load in loads[:4]:
        load.wait()
    t = tmpl[...]
    t = t - jnp.sum(t, keepdims=True) * (1.0 / (PROJ * PROJ))
    spread = jnp.sum(t * t, keepdims=True) * (1.0 / (PROJ * PROJ))
    t = t / jnp.sqrt(spread + 1e-6)
    for k, z in enumerate(second_pass(*first_pass(t[:T], t[T:], None))):
        spec[k] = z

    loads[5].wait()

    @pl.loop(0, FINE)
    def _(f):
        part = jnp.sum(fine_v[f].reshape(PROJ // 8, 8, PROJ), axis=0)
        sums[f] = part[:, :T] + part[:, T:]

    mean = jnp.sum(sums[...], axis=(1, 2), keepdims=True) * (1.0 / (PROJ * PROJ))
    sums[...] = jnp.broadcast_to(mean, (FINE, 8, T))

    pl.semaphore_wait(near_sem, 2)
    for peer in (other(4), other(12)):
        pl.semaphore_signal(mid_sem, inc=1, device_id=(peer, r, c), device_id_type=MESH)

    @pl.loop(0, FINE // 2)
    def _(pair):
        at = pl.ds(pl.multiple_of(pair * 16, 16), 16)
        below = pl.ds(pl.multiple_of(pair * 16 + T, 16), 16)
        mean = jnp.concatenate([sums[pair * 2], sums[pair * 2 + 1]], axis=0)
        mean = jnp.concatenate([mean, mean], axis=1)
        total = jnp.zeros((16, PROJ), F32)
        for i in range(PROJ // 8):
            group = pl.ds(i * 8, 8)
            x = jnp.concatenate([fine_v[pair * 2, group], fine_v[pair * 2 + 1, group]], axis=0) - mean
            total = total + x * x
            high, low = split(x)
            planes[at, pl.ds(i * PROJ, PROJ)] = high
            planes[below, pl.ds(i * PROJ, PROJ)] = low
        squares_v[at] = total[:, :T] + total[:, T:]

    pl.semaphore_wait(mid_sem, 2)
    pl.semaphore_signal(mate_sem, inc=1, device_id=(mate, r, c), device_id_type=MESH)

    loads[4].wait()
    loads[6].wait()
    loads[7].wait()
    def arrived(columns):
        for i, (dr, dc) in enumerate(NEAR):
            if dc in columns:
                @pl.when(inside(-dr, -dc))
                def _():
                    halo(i).wait_recv()

    arrived((0,))
    middle = first_pass(*[win[1, pl.ds(k * T, T)] for k in range(3)])
    arrived((-1, 1))
    sides = first_pass(
        *[jnp.concatenate([win[j, pl.ds(k * T, T)] for j in (0, 2)], axis=1) for k in range(3)]
    )
    w = [
        jnp.concatenate([side[:, :T], mid, side[:, T:]], axis=1) for side, mid in zip(sides, middle)
    ]
    left, right = [], []
    for k, z in enumerate(second_pass(*w)):
        wr, wi = z[:, :T], z[:, T:]
        tr, ti = spec[k, :, :T], spec[k, :, T:]
        prod = jnp.concatenate([wr * tr + wi * ti, wi * tr - wr * ti], axis=1)
        terms = times_terms(prod, inv_v[k])
        left += terms[0]
        right += terms[1]
    u = joined_dot(left, right)
    u = jnp.concatenate([u[:, :T], u[:, T:]], axis=0)
    corr[...] = table_times(back_v[...], u).reshape(BANDS, BAND, T)

    def band_copy(step, owner):
        return pltpu.make_async_remote_copy(
            src_ref=corr.at[lax.div(other(step), 2)],
            dst_ref=bands.at[owner],
            send_sem=band_send.at[step],
            recv_sem=band_recv.at[step],
            device_id=(other(step), r, c),
            device_id_type=MESH,
        )

    def final_copy(step, owner):
        return pltpu.make_async_remote_copy(
            src_ref=finals.at[owner],
            dst_ref=finals.at[owner],
            send_sem=final_send.at[step],
            recv_sem=final_recv.at[step],
            device_id=(other(step), r, c),
            device_id_type=MESH,
        )

    def snr_copy(step, owner):
        return pltpu.make_async_remote_copy(
            src_ref=snr.at[owner],
            dst_ref=snr.at[owner],
            send_sem=snr_send.at[step],
            recv_sem=snr_recv.at[step],
            device_id=(other(2 * step), r, c),
            device_id_type=MESH,
        )

    pl.semaphore_wait(mate_sem, 1)
    for step in FAR_FIRST:
        band_copy(step, o).start()
    layer = lax.div(o, 2)
    bands[o] = corr[layer]

    loads[8].wait()
    loads[9].wait()
    part_lane = lax.broadcasted_iota(jnp.int32, (8, T), 1)

    @pl.loop(0, SLOTS // 2)
    def _(pair):
        at = pl.ds(pl.multiple_of(pair * 16, 16), 16)
        below = pl.ds(pl.multiple_of(pair * 16 + T, 16), 16)
        row = [rows[pair * 2 + k] for k in range(2)]
        column = [cols[pair * 2 + k] for k in range(2)]
        for i in range(PROJ // 8):
            both = []
            for k in range(2):
                shift = lax.rem(T - column[k], T)
                parts = [pltpu.roll(win[j, pl.ds(row[k] + i * 8, 8)], shift, 1) for j in range(3)]
                keep = part_lane < T - column[k]
                both.append(
                    jnp.concatenate([jnp.where(keep, parts[j], parts[j + 1]) for j in range(2)], axis=1)
                )
            high, low = split(jnp.concatenate(both, axis=0))
            patches[at, pl.ds(i * PROJ, PROJ)] = high
            patches[below, pl.ds(i * PROJ, PROJ)] = low

    scores = lax.dot_general(
        patches[...], planes[...], (((1,), (1,)), ((), ())), preferred_element_type=F32
    )
    scores = (scores[:T, :T] + (scores[:T, T:] + scores[T:, :T])) + scores[T:, T:]
    at_row = lax.broadcasted_iota(jnp.int32, (T, T), 0)
    at_lane = lax.broadcasted_iota(jnp.int32, (T, T), 1)
    scores = jnp.where(at_row % 8 == at_lane % 8, scores, 0.0)
    scores = jnp.sum(scores.reshape(SLOTS, 8, T), axis=1)
    spread = jnp.sum(squares_v[...].T, axis=0, keepdims=True)
    for far in (4, 2, 1):
        scores = scores + pltpu.roll(scores, T - far, 1)
        spread = spread + pltpu.roll(spread, T - far, 1)
    scores = scores * ((1.0 / PROJ) / jnp.sqrt(spread * (1.0 / (PROJ * PROJ)) + 1e-6))
    lane = lax.broadcasted_iota(jnp.int32, (SLOTS, T), 1)
    local = jnp.max(jnp.where(lane % 8 == 0, scores, -jnp.inf), axis=1, keepdims=True)
    local = jnp.broadcast_to(local, (SLOTS, T))
    at_row = lax.broadcasted_iota(jnp.int32, (SLOTS, T), 0)
    at_lane = lax.broadcasted_iota(jnp.int32, (SLOTS, T), 1)
    local = jnp.sum(jnp.where(at_row == at_lane, local, 0.0), axis=0, keepdims=True)
    finals[o] = jnp.broadcast_to(local, (8, T))
    for step in FAR_FIRST:
        final_copy(step, o).start()

    for step in FAR_FIRST:
        band_copy(step, other(-step)).wait_recv()
    best = bands[0]
    added = bands[0]
    squares = bands[0] * bands[0]
    for k in range(1, GROUP):
        value = bands[k]
        best = jnp.maximum(best, value)
        added = added + value
        squares = squares + value * value
    snr[layer] = (best - added / GROUP) / jnp.sqrt(squares / GROUP + 1e-5)
    for step in ALONG_Z:
        snr_copy(step, layer).start()

    for step in FAR_FIRST:
        final_copy(step, other(-step)).wait_recv()
    best_fine = finals[0]
    for k in range(1, GROUP):
        best_fine = jnp.maximum(best_fine, finals[k])
    loads[10].wait()
    slot = lax.broadcasted_iota(jnp.int32, (8, T), 1)
    best_out[...] = jnp.where(slot < count[0], best_fine, 0.0)

    for step in ALONG_Z:
        snr_copy(step, lax.div(other(-2 * step), 2)).wait_recv()
    snr_out[...] = snr[...].reshape(T, T)

    for i, (dr, dc) in enumerate(NEAR):
        @pl.when(inside(dr, dc))
        def _():
            halo(i).wait_send()
    for step in FAR_FIRST:
        band_copy(step, o).wait_send()
        final_copy(step, o).wait_send()
    for step in ALONG_Z:
        snr_copy(step, layer).wait_send()


def in_hbm(x):
    return pltpu.with_memory_space_constraint(x, pltpu.HBM)


def finish(snr, best, snr_out, refined):
    snr_out[...] = snr[...]
    refined[...] = best[0, :SLOTS]


def per_device(micrograph, templates, fine_templates, peak_rows, peak_cols, peak_count):
    consts = [in_hbm(jnp.asarray(x)) for x in tables()]
    arrays = [in_hbm(x) for x in (micrograph, templates, fine_templates, peak_rows, peak_cols)]
    any_spec = pl.BlockSpec(memory_space=pl.ANY)
    vmem = pl.BlockSpec(memory_space=pltpu.VMEM)
    dma = pltpu.SemaphoreType.DMA
    regular = pltpu.SemaphoreType.REGULAR
    snr, best = pl.pallas_call(
        kernel,
        out_shape=(
            jax.ShapeDtypeStruct((T, T), F32),
            jax.ShapeDtypeStruct((8, T), F32),
        ),
        in_specs=[any_spec] * 11,
        out_specs=(vmem, vmem),
        scratch_shapes=[
            pltpu.VMEM((3, LEN, T), F32),
            pltpu.VMEM((PROJ, PROJ), F32),
            pltpu.VMEM((FINE, PROJ, PROJ), F32),
            pltpu.VMEM((2 * T, 4 * T), BF16),
            pltpu.VMEM((T, 2 * T), BF16),
            pltpu.VMEM((3, 4 * T, 2 * T), BF16),
            pltpu.VMEM((3, 4 * T, 2 * T), BF16),
            pltpu.VMEM((T, 2 * LEN), BF16),
            pltpu.VMEM((3, LEN // 2, 2 * T), F32),
            pltpu.VMEM((FINE, 8, T), F32),
            pltpu.VMEM((FINE * 8, T), F32),
            pltpu.VMEM((PROJ, PROJ * PROJ // 8), BF16),
            pltpu.VMEM((PROJ, PROJ * PROJ // 8), BF16),
            pltpu.VMEM((BANDS, BAND, T), F32),
            pltpu.VMEM((GROUP, BAND, T), F32),
            pltpu.VMEM((BANDS, BAND, T), F32),
            pltpu.VMEM((GROUP, 8, T), F32),
            pltpu.SMEM((SLOTS,), jnp.int32),
            pltpu.SMEM((SLOTS,), jnp.int32),
            pltpu.SMEM((1,), jnp.int32),
            dma((11,)),
            dma((8,)),
            dma((8,)),
            dma((16,)),
            dma((16,)),
            dma((16,)),
            dma((16,)),
            dma((16,)),
            dma((16,)),
            regular,
            regular,
            regular,
        ],
        compiler_params=pltpu.CompilerParams(
            collective_id=0, has_side_effects=True, vmem_limit_bytes=48 * 1024 * 1024
        ),
    )(*arrays, peak_count, *consts)
    return pl.pallas_call(
        finish,
        out_shape=(jax.ShapeDtypeStruct((T, T), F32), jax.ShapeDtypeStruct((SLOTS,), F32)),
        in_specs=[vmem, vmem],
        out_specs=(vmem, vmem),
        compiler_params=pltpu.CompilerParams(vmem_limit_bytes=1024 * 1024),
    )(snr, best)


def solution(mesh):
    placed = (
        P("trow", "tcol"),
        P("orient", None, None),
        P("orient", None, None),
        P(("trow", "tcol")),
        P(("trow", "tcol")),
        P(("trow", "tcol")),
    )
    return jax.shard_map(
        per_device,
        mesh=mesh,
        in_specs=placed,
        out_specs=(P("trow", "tcol"), P(("trow", "tcol"))),
        check_vma=False,
    )
```
